512 devices in a mesh: gx: 32 (over y, x, core), gy: 16 (over z).
Axes of the slice: x: 4, y: 4, z: 16, core: 2. Of those that a mesh axis runs over, the one named last changes fastest.
Arguments:
- velocity: float32 [3, 512, 512, 256], P(None, 'gx', 'gy'), may hold values from -6 to 6
- refine_flags: int32 [3, 64, 64], P(None, 'gx', 'gy'), may hold values 0 or 1
- metric_table: float32 [3, 64], replicated, may hold values from 0.25 to 2.5
- index_x: int32 [512], P('gx'), may hold values from 0 to 63
- index_y: int32 [512], P('gy'), may hold values from 0 to 63
- index_z: int32 [256], replicated, may hold values from 0 to 63
Outputs:
- details_one: float32 [3, 7, 256, 256, 128], P(None, None, 'gx', 'gy')
- details_two: float32 [3, 7, 128, 128, 64], P(None, None, 'gx', 'gy')
- details_three: float32 [3, 7, 64, 64, 32], P(None, None, 'gx', 'gy')
- coarse: float32 [3, 64, 64, 32], P(None, 'gx', 'gy')
The draws below stay inside these ranges and needn't reach their ends.
All inputs are finite; a program needn't handle non-finite values. No bound on the sum of `refine_flags` on one device may be relied on, other than what follows from the above.
Results may differ from the reference program's by a relative error of at most 0.00002.
Values sent between devices are 32-bit elements; how exact they have to be, the bound alone decides.
A program may use at most 64 MiB of HBM per device.

```python
import math
import jax
import jax.numpy as jnp
from jax import lax

NZ = 256
LEVELS = 3
BLOCK = 8
CLASSES = 64
NX = 512
NY = 512


def place_ends(result, key, least, top_value):
    index_at = [jax.random.randint(jax.random.fold_in(key, axis), (), 0, length) for axis, length in enumerate(result.shape)]
    widest = result.shape.index(max(result.shape))
    next_to = index_at[:widest] + [(index_at[widest] + 1) % result.shape[widest]] + index_at[widest + 1:]
    return result.at[tuple(index_at)].set(least).at[tuple(next_to)].set(top_value)


def steps_of(stream_key, shape, cuts, low, top_value):
    def one(axis_at, blocks):
        heights = jax.random.uniform(jax.random.fold_in(jax.random.fold_in(stream_key, 6), axis_at), (blocks,), jnp.float32, low / len(cuts), top_value / len(cuts))
        return jnp.repeat(jnp.exp(heights), shape[axis_at] // blocks).reshape((-1,) + (1,) * (len(shape) - axis_at - 1))

    loudness = one(*cuts[0])
    for cut in cuts[1:]:
        loudness = loudness * one(*cut)
    return loudness


def normal_values(own_key, extent, spread, most, cuts=(), kind=jnp.bfloat16):
    array = jax.random.normal(own_key, extent, jnp.float32) * spread
    if len(cuts) > 0:
        array = steps_of(own_key, extent, cuts, -0.22, 0.18) * array
    return jnp.clip(array, min=-most, max=most).astype(kind)


def setup_inputs(seed: int = 0) -> dict:
    keys = jax.random.split(jax.random.key(seed), 7)
    velocity = normal_values(keys[0], (3, NX, NY, NZ), 1.0, 6.0, ((1, 32), (2, 16)), jnp.float32)
    refine_flags = place_ends((jax.random.randint(keys[1], (LEVELS, NX // BLOCK, NY // BLOCK), 0, 4) < 3).astype(jnp.int32), jax.random.fold_in(keys[1], 1), 0, 1)
    metric_table = jnp.clip(jnp.exp(jax.random.uniform(keys[2], (3, CLASSES), jnp.float32, math.log(0.25), math.log(2.5))), 0.25, 2.5)
    index_x = place_ends(jax.random.randint(keys[3], (NX,), 0, CLASSES), jax.random.fold_in(keys[3], 1), 0, CLASSES - 1).astype(jnp.int32)
    index_y = place_ends(jax.random.randint(keys[4], (NY,), 0, CLASSES), jax.random.fold_in(keys[4], 1), 0, CLASSES - 1).astype(jnp.int32)
    index_z = place_ends(jax.random.randint(keys[5], (NZ,), 0, CLASSES), jax.random.fold_in(keys[5], 1), 0, CLASSES - 1).astype(jnp.int32)
    return {"velocity": velocity, "refine_flags": refine_flags, "metric_table": metric_table, "index_x": index_x, "index_y": index_y, "index_z": index_z}


def periodic_ext(values, axis_no, width):
    length = values.shape[axis_no]
    head_part = lax.slice_in_dim(values, length - width, length, axis=axis_no)
    tail_part = lax.slice_in_dim(values, 0, width, axis=axis_no)
    return jnp.concatenate([head_part, values, tail_part], axis=axis_no)


def central(extended, axis_no, length):
    return lax.slice_in_dim(extended, 2, length + 2, axis=axis_no) - lax.slice_in_dim(extended, 0, length, axis=axis_no)


def even_odd(values, axis_no):
    length = values.shape[axis_no]
    even_part = lax.slice_in_dim(values, 0, length, stride=2, axis=axis_no)
    odd_part = lax.slice_in_dim(values, 1, length, stride=2, axis=axis_no)
    return even_part, odd_part


def predict_step(even_ext, odd_part, axis_no, keep_mask):
    length = odd_part.shape[axis_no]
    left_one = lax.slice_in_dim(even_ext, 1, length + 1, axis=axis_no)
    centre = lax.slice_in_dim(even_ext, 2, length + 2, axis=axis_no)
    right_one = lax.slice_in_dim(even_ext, 3, length + 3, axis=axis_no)
    right_two = lax.slice_in_dim(even_ext, 4, length + 4, axis=axis_no)
    return (odd_part - (9.0 * (centre + right_one) - (left_one + right_two)) / 16.0) * keep_mask


def update_step(even_part, detail_ext, axis_no):
    length = even_part.shape[axis_no]
    left_two = lax.slice_in_dim(detail_ext, 0, length, axis=axis_no)
    left_one = lax.slice_in_dim(detail_ext, 1, length + 1, axis=axis_no)
    centre = lax.slice_in_dim(detail_ext, 2, length + 2, axis=axis_no)
    right_one = lax.slice_in_dim(detail_ext, 3, length + 3, axis=axis_no)
    return even_part + (9.0 * (left_one + centre) - (left_two + right_one)) / 32.0


def lift_local(values, axis_no, keep_mask):
    even_part, odd_part = even_odd(values, axis_no)
    detail = predict_step(periodic_ext(even_part, axis_no, 2), odd_part, axis_no, keep_mask)
    smooth = update_step(even_part, periodic_ext(detail, axis_no, 2), axis_no)
    return smooth, detail


def level_mask(flag_plane, rep_x, rep_y):
    return jnp.repeat(jnp.repeat(flag_plane, rep_x, axis=0), rep_y, axis=1).astype(jnp.float32)


def reference(velocity, refine_flags, metric_table, index_x, index_y, index_z):
    metric_x = metric_table[0][index_x]
    metric_y = metric_table[1][index_y]
    metric_z = metric_table[2][index_z]
    diff_x = central(periodic_ext(velocity, 1, 1), 1, velocity.shape[1]) * metric_x[None, :, None, None]
    diff_y = central(periodic_ext(velocity, 2, 1), 2, velocity.shape[2]) * metric_y[None, None, :, None]
    diff_z = central(periodic_ext(velocity, 3, 1), 3, velocity.shape[3]) * metric_z[None, None, None, :]
    vort_x = diff_y[2] - diff_z[1]
    vort_y = diff_z[0] - diff_x[2]
    vort_z = diff_x[1] - diff_y[0]
    current = jnp.stack([vort_x, vort_y, vort_z])
    results = []
    for level_idx in range(LEVELS):
        repeat_no = BLOCK // 2 ** (level_idx + 1)
        flag_plane = refine_flags[level_idx]
        plane_x = level_mask(flag_plane, repeat_no, 2 * repeat_no)
        plane_yz = level_mask(flag_plane, repeat_no, repeat_no)
        smooth, detail = lift_local(current, 1, plane_x[None, :, :, None])
        halfway = jnp.stack([smooth, detail], axis=1)
        smooth, detail = lift_local(halfway, 3, plane_yz[None, None, :, :, None])
        halfway = jnp.stack([smooth, detail], axis=2)
        smooth, detail = lift_local(halfway, 5, plane_yz[None, None, None, :, :, None])
        stacked = jnp.stack([smooth, detail], axis=3)
        bands = stacked.reshape((3, 8) + stacked.shape[4:])
        results.append(bands[:, 1:])
        current = bands[:, 0]
    return results[0], results[1], results[2], current
```

```python
import functools

import jax
import jax.numpy as jnp
import numpy as np
from jax import lax
from jax.experimental import pallas as pl
from jax.experimental.pallas import tpu as pltpu
from jax.sharding import PartitionSpec as P

F32 = jnp.float32
BF16 = jnp.bfloat16
NX = (16, 8, 4)
NY = (32, 16, 8)
ZH = (2, 1, 1)
REP = (4, 2, 1)
DR = (24, 16, 8)
XK_LOW = (-1, -1, -2)
OWN, XL, XR, YL, YR = range(5)


def z_matrices(count):
    half = count // 2
    even = np.zeros((count, half))
    residual = np.zeros((count, half))
    for k in range(half):
        even[2 * k, k] = 1.0
        residual[2 * k + 1, k] += 1.0
        for at, weight in ((k, -9), (k + 1, -9), (k - 1, 1), (k + 2, 1)):
            residual[2 * (at % half), k] += weight / 16.0
    update = np.zeros((count, half))
    for k in range(half):
        for at, weight in ((k - 1, 9), (k, 9), (k - 2, -1), (k + 1, -1)):
            update[:, k] += weight / 32.0 * residual[:, at % half]
    rows = max(count, 128)
    full = np.zeros((rows, 3, 128))
    for part, matrix in enumerate((even, residual, update)):
        full[:count, part, :half] = matrix
    return full.reshape(rows, 384)


def kernel(
    vel_hbm, flags, table, ix, iy, iz_ref, w1_hbm, w2_hbm, w3_hbm,
    o1_hbm, o2_hbm, o3_hbm, oc_hbm,
    vel, hy, c1, c2, c3, x1, x2, x3, y1, y2, y3, dscr,
    mk, mx1, mx2, mx3, my1, my2, my3, mz1, mz2, mz3, myt, mzt,
    w1, w2, w3, o1, o2, o3, oc,
    send_sem, recv_sem, local_sem,
):
    C, X, Y = (c1, c2, c3), (x1, x2, x3), (y1, y2, y3)
    MX, MY, MZ, W = (mx1, mx2, mx3), (my1, my2, my3), (mz1, mz2, mz3), (w1, w2, w3)
    gx, gy = lax.axis_index("gx"), lax.axis_index("gy")
    nx, ny = lax.axis_size("gx"), lax.axis_size("gy")
    right, left = {"gx": lax.rem(gx + 1, nx)}, {"gx": lax.rem(gx + nx - 1, nx)}
    right2, left2 = {"gx": lax.rem(gx + 2, nx)}, {"gx": lax.rem(gx + nx - 2, nx)}
    up, down = {"gy": lax.rem(gy + 1, ny)}, {"gy": lax.rem(gy + ny - 1, ny)}

    counter = [0]
    pending = []

    def remote(src, dst, device):
        n = counter[0]
        counter[0] += 1
        copy = pltpu.make_async_remote_copy(
            src_ref=src, dst_ref=dst, send_sem=send_sem.at[n], recv_sem=recv_sem.at[n],
            device_id=device, device_id_type=pl.DeviceIdType.MESH,
        )
        copy.start()
        pending.append(copy)
        return copy

    def wait_recv(copies):
        for copy in copies:
            copy.wait_recv()

    local = [
        pltpu.make_async_copy(vel_hbm, vel.at[:, pl.ds(1, 16)], local_sem.at[0]),
        pltpu.make_async_copy(w1_hbm, w1, local_sem.at[1]),
        pltpu.make_async_copy(w2_hbm, w2, local_sem.at[2]),
        pltpu.make_async_copy(w3_hbm, w3, local_sem.at[3]),
    ]
    for copy in local:
        copy.start()

    barrier = pltpu.get_barrier_semaphore()
    for device in (right, left, right2, left2, up, down):
        pl.semaphore_signal(barrier, inc=1, device_id=device, device_id_type=pl.DeviceIdType.MESH)

    for l in range(3):
        for bx in range(2):
            for by in range(4):
                mk[OWN, l, bx, pl.ds(by, 1), :] = jnp.full((1, 128), flags[l, bx, by].astype(F32), F32)
    for j in range(32):
        myt[pl.ds(j, 1), :] = jnp.full((1, 128), table[1, iy[j]], F32)
    iz = iz_ref[...]

    def z_class(c, total):
        return jnp.where(iz == c, table[2, c], total)

    mzt[...] = lax.fori_loop(0, 64, z_class, jnp.zeros((1, 256), F32))

    pl.semaphore_wait(barrier, 6)

    r0 = [
        remote(vel_hbm.at[pl.ds(1, 2), pl.ds(15, 1)], vel.at[pl.ds(1, 2), pl.ds(0, 1)], right),
        remote(vel_hbm.at[pl.ds(1, 2), pl.ds(0, 1)], vel.at[pl.ds(1, 2), pl.ds(17, 1)], left),
    ]
    for at, comp in enumerate((0, 2)):
        r0.append(remote(vel_hbm.at[comp, :, 31], hy.at[0, at], up))
        r0.append(remote(vel_hbm.at[comp, :, 0], hy.at[1, at], down))
    m0 = [
        remote(mk.at[OWN], mk.at[XL], right),
        remote(mk.at[OWN], mk.at[XR], left),
        remote(mk.at[OWN], mk.at[YL], up),
        remote(mk.at[OWN], mk.at[YR], down),
    ]
    local[0].wait()
    wait_recv(r0)

    row = lax.broadcasted_iota(jnp.int32, (32, 256), 0)

    def vorticity(i, carry):
        mx = table[0, ix[i]]
        u, v, w = vel[0, i + 1], vel[1, i + 1], vel[2, i + 1]
        my = jnp.concatenate([myt[...], myt[...]], axis=1)
        mz = mzt[...]

        def along_y(f, at):
            before = jnp.where(row == 0, hy[0, at, pl.ds(i, 1), :], pltpu.roll(f, 1, 0))
            after = jnp.where(row == 31, hy[1, at, pl.ds(i, 1), :], pltpu.roll(f, 31, 0))
            return (after - before) * my

        def along_z(f):
            return (pltpu.roll(f, 255, 1) - pltpu.roll(f, 1, 1)) * mz

        dv_dx = (vel[1, i + 2] - vel[1, i]) * mx
        dw_dx = (vel[2, i + 2] - vel[2, i]) * mx
        curl = (along_y(w, 1) - along_z(v), along_z(u) - dw_dx, dv_dx - along_y(u, 0))
        for c in range(3):
            for h in range(2):
                c1[c, h, i + 6] = curl[c][:, 128 * h : 128 * (h + 1)]
        return carry

    lax.fori_loop(10, 16, vorticity, 0)
    lax.fori_loop(0, 5, vorticity, 0)

    def send_x(l, comps):
        n = NX[l]
        src = lambda start, size: C[l].at[comps, :, pl.ds(start + 6, size)]
        if l < 2:
            return [
                remote(src(n - 6, 1), src(-6, 1), right),
                remote(src(n - 4, 4), src(-4, 4), right),
                remote(src(0, 3), src(n, 3), left),
                remote(src(4, 1), src(n + 4, 1), left),
            ]
        return [
            remote(src(0, 4), src(-4, 4), right),
            remote(src(2, 1), src(-6, 1), right2),
            remote(src(0, 3), src(4, 3), left),
            remote(src(0, 1), src(8, 1), left2),
        ]

    def send_y(l, comps, a):
        n = NY[l]
        part = lambda start: X[l].at[comps, :, a, :, pl.ds(start + 8, 8)]
        return [remote(part(n - 8), part(-8), up), remote(part(0), part(n), down)]

    def lift_x(l, comps):
        half = NX[l] // 2
        tiles = NY[l] // 8

        def body(it, carry):
            h, t = it // tiles, lax.rem(it, tiles)
            rows = pl.ds(pl.multiple_of(t * 8, 8), 8)
            rows_to = pl.ds(pl.multiple_of(t * 8 + 8, 8), 8)
            for c in comps:
                p = lambda i: C[l][c, h, i + 6, rows, :]
                d = {}
                for k in range(-2, half + 1):
                    mask = MX[l][k // REP[l] - XK_LOW[l], rows, :]
                    d[k] = (p(2 * k + 1) - (9.0 * (p(2 * k) + p(2 * k + 2)) - (p(2 * k - 2) + p(2 * k + 4))) * 0.0625) * mask
                for k in range(half):
                    smooth = p(2 * k) + (9.0 * (d[k - 1] + d[k]) - (d[k - 2] + d[k + 1])) * 0.03125
                    X[l][c, h, 0, k, rows_to, :] = smooth
                    X[l][c, h, 1, k, rows_to, :] = d[k]
            return carry

        lax.fori_loop(0, ZH[l] * tiles, body, 0)

    def lift_y(l, c, a):
        half_x, n, r = NX[l] // 2, NY[l] // 2, DR[l]

        def body(h, carry):
            for k in range(half_x):
                line = lambda start, count: X[l][c, h, a, k, pl.ds(start + 8, count, stride=2), :]
                mask = MY[l][k // REP[l]]
                d = (line(-3, r) - (9.0 * (line(-4, r) + line(-2, r)) - (line(-6, r) + line(0, r))) * 0.0625) * mask
                dscr[k, 0:r] = d
                part = lambda s: dscr[k, s : s + n]
                own = part(2)
                smooth = line(0, n) + (9.0 * (part(1) + own) - (part(0) + part(3))) * 0.03125
                at = (c * half_x + k) * n
                Y[l][2 * a, h, at : at + n] = smooth
                Y[l][2 * a + 1, h, at : at + n] = own
            return carry

        lax.fori_loop(0, ZH[l], body, 0)

    def lift_z(l, c, ab):
        half_x, n = NX[l] // 2, NY[l] // 2
        size = half_x * n
        acc = None
        for h in range(ZH[l]):
            x = Y[l][ab, h, c * size : (c + 1) * size, :]
            weights = W[l][h * 128 : (h + 1) * 128, :]
            hi = x.astype(BF16)
            rest = x - hi.astype(F32)
            mid = rest.astype(BF16)
            low = (rest - mid.astype(F32)).astype(BF16)
            for piece in (low, mid, hi):
                term = jnp.dot(piece, weights, preferred_element_type=F32)
                acc = term if acc is None else acc + term
        mask = MZ[l][...]
        smooth = acc[:, :128] + mask * acc[:, 256:]
        detail = mask * acc[:, 128:256]
        lanes = (128, 64, 32)[l]
        out = (o1, o2, o3)[l]
        for k in range(half_x):
            rows = slice(k * n, (k + 1) * n)
            out[c, 2 * ab, k] = detail[rows, :lanes]
            if ab > 0:
                out[c, 2 * ab - 1, k] = smooth[rows, :lanes]
            elif l < 2:
                C[l + 1][c, 0, k + 6] = smooth[rows]
            else:
                oc[c, k] = smooth[rows, :lanes]

    everything = (0, 1, 2)
    all_comps = pl.ds(0, 3)
    x_in = [send_x(0, c) for c in everything]
    lax.fori_loop(5, 10, vorticity, 0)

    wait_recv(m0)
    for l in range(3):
        per = 2 * REP[l]
        for at in range(MX[l].shape[0]):
            bx = at + XK_LOW[l]
            slot = XL if bx < 0 else XR if bx > 1 else OWN
            for by in range(4):
                MX[l][at, pl.ds(by * per, per), :] = jnp.broadcast_to(mk[slot, l, bx % 2, pl.ds(by, 1), :], (per, 128))
        n = NY[l] // 2
        for bx in range(2):
            for m in range(-2, DR[l] - 2):
                by = min(m // REP[l], 4)
                slot = YL if by < 0 else YR if by > 3 else OWN
                MY[l][bx, pl.ds(m + 2, 1), :] = mk[slot, l, bx, pl.ds(by % 4, 1), :]
        for k in range(NX[l] // 2):
            MZ[l][k * n : (k + 1) * n] = MY[l][k // REP[l], 2 : 2 + n]
    for copy in local[1:]:
        copy.wait()

    y_in = []
    for c in everything:
        wait_recv(x_in[c])
        lift_x(0, (c,))
        y_in.append([send_y(0, c, a) for a in range(2)])
    for c in everything:
        wait_recv(y_in[c][0])
        lift_y(0, c, 0)
        lift_z(0, c, 0)
    x_in2 = send_x(1, all_comps)
    for c in everything:
        lift_z(0, c, 1)
    wait_recv(x_in2)
    lift_x(1, everything)
    y_in2 = [send_y(1, all_comps, a) for a in range(2)]
    for c in everything:
        wait_recv(y_in[c][1])
        lift_y(0, c, 1)
    for a in range(2):
        wait_recv(y_in2[a])
    for c in everything:
        lift_y(1, c, 0)
        lift_z(1, c, 0)
    x_in3 = send_x(2, all_comps)
    for c in everything:
        lift_y(1, c, 1)
        for ab in range(1, 4):
            lift_z(1, c, ab)
        lift_z(0, c, 2)
    outs = [pltpu.make_async_copy(o2, o2_hbm, local_sem.at[5])]
    outs[0].start()
    wait_recv(x_in3)
    lift_x(2, everything)
    y_in3 = [send_y(2, all_comps, a) for a in range(2)]
    for c in everything:
        lift_z(0, c, 3)
    outs.append(pltpu.make_async_copy(o1, o1_hbm, local_sem.at[4]))
    outs[1].start()
    for a in range(2):
        wait_recv(y_in3[a])
    for c in everything:
        for a in range(2):
            lift_y(2, c, a)
        for ab in range(4):
            lift_z(2, c, ab)
    outs.append(pltpu.make_async_copy(o3, o3_hbm, local_sem.at[6]))
    outs.append(pltpu.make_async_copy(oc, oc_hbm, local_sem.at[7]))
    for copy in outs[2:]:
        copy.start()
    for copy in pending:
        copy.wait_send()
    for copy in outs:
        copy.wait()


def on_device(velocity, refine_flags, metric_table, index_x, index_y, index_z):
    weights = [jnp.asarray(z_matrices(count).astype(np.float32)).astype(BF16) for count in (256, 128, 64)]
    anywhere = pl.BlockSpec(memory_space=pl.ANY)
    smem = pl.BlockSpec(memory_space=pltpu.SMEM)
    vmem = pl.BlockSpec(memory_space=pltpu.VMEM)
    out_shapes = [(3, 7, 8, 16, 128), (3, 7, 4, 8, 64), (3, 7, 2, 4, 32), (3, 2, 4, 32)]
    v = pltpu.VMEM
    scratch = [v((3, 18, 32, 256), F32), v((2, 2, 16, 256), F32)]
    scratch += [v((3, ZH[l], NX[l] + 11, NY[l], 128), F32) for l in range(3)]
    scratch += [v((3, ZH[l], 2, NX[l] // 2, NY[l] + 24, 128), F32) for l in range(3)]
    scratch += [v((4, ZH[l], 3 * NX[l] * NY[l] // 4, 128), F32) for l in range(3)]
    scratch += [v((8, 32, 128), F32), v((5, 3, 2, 8, 128), F32)]
    scratch += [v((4 if l < 2 else 5, NY[l], 128), F32) for l in range(3)]
    scratch += [v((2, DR[l], 128), F32) for l in range(3)]
    scratch += [v((NX[l] * NY[l] // 4, 128), F32) for l in range(3)]
    scratch += [v((32, 128), F32), v((1, 256), F32)]
    scratch += [v((256, 384), BF16), v((128, 384), BF16), v((128, 384), BF16)]
    scratch += [v(shape, F32) for shape in out_shapes]
    scratch += [pltpu.SemaphoreType.DMA((64,)), pltpu.SemaphoreType.DMA((64,)), pltpu.SemaphoreType.DMA((8,))]
    return pl.pallas_call(
        kernel,
        out_shape=[jax.ShapeDtypeStruct(shape, F32) for shape in out_shapes],
        in_specs=[anywhere, smem, smem, smem, smem, vmem, anywhere, anywhere, anywhere],
        out_specs=[anywhere] * 4,
        scratch_shapes=scratch,
        compiler_params=pltpu.CompilerParams(collective_id=0, has_side_effects=True),
        name="analysis",
    )(velocity, refine_flags, metric_table, index_x, index_y, index_z.reshape(1, 256), *weights)


def solution(mesh):
    return jax.shard_map(
        on_device,
        mesh=mesh,
        in_specs=(P(None, "gx", "gy", None), P(None, "gx", "gy"), P(), P("gx"), P("gy"), P()),
        out_specs=(
            P(None, None, "gx", "gy", None),
            P(None, None, "gx", "gy", None),
            P(None, None, "gx", "gy", None),
            P(None, "gx", "gy", None),
        ),
        check_vma=False,
    )
```

```python
import functools

import jax
import jax.numpy as jnp
import numpy as np
from jax import lax
from jax.experimental import pallas as pl
from jax.experimental.pallas import tpu as pltpu
from jax.sharding import PartitionSpec as P

F32 = jnp.float32
BF16 = jnp.bfloat16
NX = (16, 8, 4)
NY = (32, 16, 8)
ZH = (2, 1, 1)
REP = (4, 2, 1)
DR = (24, 16, 8)
XK_LOW = (-1, -1, -2)
ROWS = (0, 8, 8)


def slot(sx, sy):
    return 3 * (sx + 1) + sy + 1


def z_matrices(count):
    half = count // 2
    even = np.zeros((count, half))
    residual = np.zeros((count, half))
    for k in range(half):
        even[2 * k, k] = 1.0
        residual[2 * k + 1, k] += 1.0
        for at, weight in ((k, -9), (k + 1, -9), (k - 1, 1), (k + 2, 1)):
            residual[2 * (at % half), k] += weight / 16.0
    update = np.zeros((count, half))
    for k in range(half):
        for at, weight in ((k - 1, 9), (k, 9), (k - 2, -1), (k + 1, -1)):
            update[:, k] += weight / 32.0 * residual[:, at % half]
    rows = max(count, 128)
    full = np.zeros((rows, 3, 128))
    for part, matrix in enumerate((even, residual, update)):
        full[:count, part, :half] = matrix
    return full.reshape(rows, 384)


def kernel(
    vel_hbm, flags, table, ix, iy, iz_ref, w1_hbm, w2_hbm, w3_hbm,
    o1, o2, o3, oc,
    vel, hy, c1, c2, c3, x1, x2, x3, y1, y2, y3, dscr,
    mk, mx1, mx2, mx3, my1, my2, my3, mz1, mz2, mz3, mxt, myt, mzt,
    w1, w2, w3,
    send_sem, recv_sem, local_sem,
):
    C, X, Y = (c1, c2, c3), (x1, x2, x3), (y1, y2, y3)
    MX, MY, MZ, W = (mx1, mx2, mx3), (my1, my2, my3), (mz1, mz2, mz3), (w1, w2, w3)
    gx, gy = lax.axis_index("gx"), lax.axis_index("gy")
    nx, ny = lax.axis_size("gx"), lax.axis_size("gy")

    def at(dx, dy):
        return {"gx": lax.rem(gx + (nx + dx), nx), "gy": lax.rem(gy + (ny + dy), ny)}

    counter = [0]
    pending = []

    def remote(src, dst, device):
        n = counter[0]
        counter[0] += 1
        copy = pltpu.make_async_remote_copy(
            src_ref=src, dst_ref=dst, send_sem=send_sem.at[n], recv_sem=recv_sem.at[n],
            device_id=device, device_id_type=pl.DeviceIdType.MESH,
        )
        copy.start()
        pending.append(copy)
        return copy

    def wait_recv(copies):
        for copy in copies:
            copy.wait_recv()

    local = [
        pltpu.make_async_copy(vel_hbm, vel.at[:, pl.ds(7, 16)], local_sem.at[0]),
        pltpu.make_async_copy(w1_hbm, w1, local_sem.at[1]),
        pltpu.make_async_copy(w2_hbm, w2, local_sem.at[2]),
        pltpu.make_async_copy(w3_hbm, w3, local_sem.at[3]),
    ]
    for copy in local:
        copy.start()

    around = [(dx, dy) for dx in (-2, -1, 0, 1, 2) for dy in (-1, 0, 1) if (dx, dy) != (0, 0)]
    barrier = pltpu.get_barrier_semaphore()
    for step in around:
        pl.semaphore_signal(barrier, inc=1, device_id=at(*step), device_id_type=pl.DeviceIdType.MESH)

    own = slot(0, 0)
    for l in range(3):
        for bx in range(2):
            for by in range(4):
                mk[own, l, bx, pl.ds(by, 1), :] = jnp.full((1, 128), flags[l, bx, by].astype(F32), F32)
    for i in range(16):
        mxt[pl.ds(i + 6, 1), :] = jnp.full((1, 128), table[0, ix[i]], F32)
    for j in range(32):
        myt[pl.ds(j, 1), :] = jnp.full((1, 128), table[1, iy[j]], F32)
    iz = iz_ref[...]

    def z_class(c, total):
        return jnp.where(iz == c, table[2, c], total)

    mzt[...] = lax.fori_loop(0, 64, z_class, jnp.zeros((1, 256), F32))

    pl.semaphore_wait(barrier, len(around))

    def send_rows(dx, dy, place, line):
        start, size, to = ((0, 8, 24), (0, 16, 8), (8, 8, 0))[dx + 1]
        return remote(vel_hbm.at[:, pl.ds(start, size), line], hy.at[place, :, pl.ds(to, size)], at(dx, dy))

    corner_rows = [send_rows(dx, dy, place, line) for dx in (1, -1) for dy, place, line in ((1, 0, 31), (-1, 1, 0))]
    own_rows = [send_rows(0, 1, 0, 31), send_rows(0, -1, 1, 0)]
    inner_rows = [send_rows(dx, 0, place, line) for dx in (1, -1) for place, line in ((2, 8), (3, 23))]
    metric_in = [
        remote(mxt.at[pl.ds(16, 6)], mxt.at[pl.ds(0, 6)], at(1, 0)),
        remote(mxt.at[pl.ds(6, 5)], mxt.at[pl.ds(22, 5)], at(-1, 0)),
    ]
    flags_in = [remote(mk.at[own], mk.at[slot(-dx, -dy)], at(dx, dy)) for dx, dy in around if abs(dx) < 2]

    def send_planes(first, size):
        rows = pl.ds(first, size)
        copies = []
        for dx, start, to, count in ((1, 9, -7, 7), (-1, 0, 16, 6)):
            skip = 1 if dx > 0 else 0
            copies.append(remote(
                vel_hbm.at[pl.ds(1, 2), pl.ds(start, count), rows], vel.at[pl.ds(1, 2), pl.ds(to + 7, count), rows], at(dx, 0)))
            copies.append(remote(
                vel_hbm.at[0, pl.ds(start + skip, count - 1), rows], vel.at[0, pl.ds(to + skip + 7, count - 1), rows], at(dx, 0)))
        return copies

    outer = send_planes(0, 8) + send_planes(24, 8)
    inner = send_planes(8, 16)

    row = lax.broadcasted_iota(jnp.int32, (8, 256), 0)

    def vorticity(lo, hi, tiles, halo):
        def body(i, carry):
            mx = jnp.concatenate([mxt[pl.ds(i + 6, 1), :]] * 2, axis=1)
            mz = mzt[...]
            for t in tiles:
                rows = slice(8 * t, 8 * t + 8)
                u, v, w = vel[0, i + 7, rows], vel[1, i + 7, rows], vel[2, i + 7, rows]
                my = jnp.concatenate([myt[rows, :]] * 2, axis=1)

                def along_y(f, c):
                    place = 0 if t == 0 else 3 if halo and t == 3 else None
                    first = vel[c, i + 7, 8 * t - 1 : 8 * t] if place is None else hy[place, c, pl.ds(i + 8, 1), :]
                    place = 1 if t == 3 else 2 if halo and t == 0 else None
                    last = vel[c, i + 7, 8 * t + 8 : 8 * t + 9] if place is None else hy[place, c, pl.ds(i + 8, 1), :]
                    before = jnp.where(row == 0, first, pltpu.roll(f, 1, 0))
                    after = jnp.where(row == 7, last, pltpu.roll(f, 7, 0))
                    return (after - before) * my

                def along_z(f):
                    return (pltpu.roll(f, 255, 1) - pltpu.roll(f, 1, 1)) * mz

                dv_dx = (vel[1, i + 8, rows] - vel[1, i + 6, rows]) * mx
                dw_dx = (vel[2, i + 8, rows] - vel[2, i + 6, rows]) * mx
                curl = (along_y(w, 2) - along_z(v), along_z(u) - dw_dx, dv_dx - along_y(u, 0))
                for c in range(3):
                    for h in range(2):
                        c1[c, h, i + 6, rows] = curl[c][:, 128 * h : 128 * (h + 1)]
            return carry

        lax.fori_loop(lo, hi, body, 0)

    def lift_x(l, comps, tiles):
        half = NX[l] // 2
        first, step, count = tiles

        def body(it, carry):
            h, t = it // count, first + step * lax.rem(it, count)
            rows = pl.ds(pl.multiple_of(t * 8, 8), 8)
            rows_to = pl.ds(pl.multiple_of(t * 8 + 8 - ROWS[l], 8), 8)
            for c in comps:
                p = lambda i: C[l][c, h, i + 6, rows, :]
                d = {}
                for k in range(-2, half + 1):
                    mask = MX[l][k // REP[l] - XK_LOW[l], rows, :]
                    d[k] = (p(2 * k + 1) - (9.0 * (p(2 * k) + p(2 * k + 2)) - (p(2 * k - 2) + p(2 * k + 4))) * 0.0625) * mask
                for k in range(half):
                    smooth = p(2 * k) + (9.0 * (d[k - 1] + d[k]) - (d[k - 2] + d[k + 1])) * 0.03125
                    X[l][c, h, 0, k, rows_to, :] = smooth
                    X[l][c, h, 1, k, rows_to, :] = d[k]
            return carry

        lax.fori_loop(0, ZH[l] * count, body, 0)

    def lift_y(l, c, a):
        half_x, n, r = NX[l] // 2, NY[l] // 2, DR[l]

        def body(h, carry):
            for k in range(half_x):
                line = lambda start, count: X[l][c, h, a, k, pl.ds(start + 8, count, stride=2), :]
                mask = MY[l][k // REP[l]]
                d = (line(-3, r) - (9.0 * (line(-4, r) + line(-2, r)) - (line(-6, r) + line(0, r))) * 0.0625) * mask
                dscr[k, 0:r] = d
                part = lambda s: dscr[k, s : s + n]
                own_part = part(2)
                smooth = line(0, n) + (9.0 * (part(1) + own_part) - (part(0) + part(3))) * 0.03125
                to = (c * half_x + k) * n
                Y[l][2 * a, h, to : to + n] = smooth
                Y[l][2 * a + 1, h, to : to + n] = own_part
            return carry

        lax.fori_loop(0, ZH[l], body, 0)

    def lift_z(l, ab):
        half_x, n = NX[l] // 2, NY[l] // 2
        acc = None
        for h in range(ZH[l]):
            x = Y[l][ab, h]
            weights = W[l][h * 128 : (h + 1) * 128, :]
            hi = x.astype(BF16)
            rest = x - hi.astype(F32)
            mid = rest.astype(BF16)
            low = (rest - mid.astype(F32)).astype(BF16)
            for piece in (low, mid, hi):
                term = jnp.dot(piece, weights, preferred_element_type=F32)
                acc = term if acc is None else acc + term
        mask = jnp.concatenate([MZ[l][...]] * 3, axis=0)
        smooth = acc[:, :128] + mask * acc[:, 256:]
        detail = mask * acc[:, 128:256]
        lanes = (128, 64, 32)[l]
        out = (o1, o2, o3)[l]
        for c in range(3):
            for k in range(half_x):
                rows = slice((c * half_x + k) * n, (c * half_x + k + 1) * n)
                out[c, 2 * ab, k] = detail[rows, :lanes]
                if ab > 0:
                    out[c, 2 * ab - 1, k] = smooth[rows, :lanes]
                elif l < 2:
                    C[l + 1][c, 0, k + 6, 8 : 8 + n] = smooth[rows]
                else:
                    oc[c, k] = smooth[rows, :lanes]

    def send_lines(c, a):
        return [
            remote(x1.at[c, :, a, :, pl.ds(34, 6)], x1.at[c, :, a, :, pl.ds(2, 6)], at(0, 1)),
            remote(x1.at[c, :, a, :, pl.ds(8, 5)], x1.at[c, :, a, :, pl.ds(40, 5)], at(0, -1)),
        ]

    def send_around(l):
        n, m = NX[l], NY[l]
        if l == 1:
            planes = ((1, n - 6, 1), (1, n - 4, 4), (-1, 0, 3), (-1, 4, 1))
        else:
            planes = ((1, 0, 4), (2, 2, 1), (-1, 0, 3), (-2, 0, 1))
        rows = ((1, m - 6, 6), (-1, 0, 5))
        moves = [(dx, dy, i, ci, j, cj) for dx, i, ci in planes for dy, j, cj in rows]
        moves += [(dx, 0, i, ci, 0, m) for dx, i, ci in planes]
        moves += [(0, dy, 0, n, j, cj) for dy, j, cj in rows]
        copies = []
        for dx, dy, i, ci, j, cj in moves:
            src = C[l].at[:, 0, pl.ds(i + 6, ci), pl.ds(j + 8, cj)]
            dst = C[l].at[:, 0, pl.ds(i + 6 - dx * n, ci), pl.ds(j + 8 - dy * m, cj)]
            copies.append(remote(src, dst, at(dx, dy)))
        return copies

    everything = (0, 1, 2)
    local[0].wait()
    wait_recv(own_rows)
    vorticity(1, 15, (0, 1, 2, 3), False)

    wait_recv(metric_in + flags_in)
    for l in range(3):
        per = 2 * REP[l]
        low = -ROWS[l] // per
        for k in range(MX[l].shape[0]):
            bx = k + XK_LOW[l]
            for by in range(low, NY[l] // per - low):
                place = slot(-1 if bx < 0 else 1 if bx > 1 else 0, -1 if by < 0 else 1 if by > 3 else 0)
                value = jnp.broadcast_to(mk[place, l, bx % 2, pl.ds(by % 4, 1), :], (per, 128))
                MX[l][k, pl.ds((by - low) * per, per), :] = value
        n = NY[l] // 2
        for bx in range(2):
            for m in range(-2, DR[l] - 2):
                by = min(m // REP[l], 4)
                place = slot(0, -1 if by < 0 else 1 if by > 3 else 0)
                MY[l][bx, pl.ds(m + 2, 1), :] = mk[place, l, bx, pl.ds(by % 4, 1), :]
        for k in range(NX[l] // 2):
            MZ[l][k * n : (k + 1) * n] = MY[l][k // REP[l], 2 : 2 + n]
    for copy in local[1:]:
        copy.wait()

    wait_recv(corner_rows + inner_rows + outer)
    vorticity(-6, 0, (0, 3), True)
    vorticity(0, 1, (0, 3), False)
    vorticity(15, 16, (0, 3), False)
    vorticity(16, 21, (0, 3), True)
    lines = []
    for c in everything:
        lift_x(0, (c,), (0, 3, 2))
        lines.append(send_lines(c, 0))
    wait_recv(inner)
    vorticity(-6, 0, (1, 2), True)
    vorticity(0, 1, (1, 2), False)
    vorticity(15, 16, (1, 2), False)
    vorticity(16, 21, (1, 2), True)
    for c in everything:
        lift_x(0, (c,), (1, 1, 2))
    for c in everything:
        wait_recv(lines[c])
        lift_y(0, c, 0)
    lift_z(0, 0)
    around2 = send_around(1)
    lines = [send_lines(c, 1) for c in everything]
    lift_z(0, 1)
    wait_recv(around2)
    lift_x(1, everything, (0, 1, 4))
    for c in everything:
        lift_y(1, c, 0)
    lift_z(1, 0)
    around3 = send_around(2)
    for c in everything:
        lift_y(1, c, 1)
    for ab in range(1, 4):
        lift_z(1, ab)
    for c in everything:
        wait_recv(lines[c])
        lift_y(0, c, 1)
    lift_z(0, 2)
    lift_z(0, 3)
    wait_recv(around3)
    lift_x(2, everything, (0, 1, 3))
    for c in everything:
        for a in range(2):
            lift_y(2, c, a)
    for ab in range(4):
        lift_z(2, ab)
    for copy in pending:
        copy.wait_send()


def write_out(*refs):
    sem = refs[8]
    copies = [pltpu.make_async_copy(refs[n], refs[4 + n], sem.at[n]) for n in range(4)]
    for copy in copies:
        copy.start()
    for copy in copies:
        copy.wait()


def on_device(velocity, refine_flags, metric_table, index_x, index_y, index_z):
    weights = [jnp.asarray(z_matrices(count).astype(np.float32)).astype(BF16) for count in (256, 128, 64)]
    anywhere = pl.BlockSpec(memory_space=pl.ANY)
    smem = pl.BlockSpec(memory_space=pltpu.SMEM)
    vmem = pl.BlockSpec(memory_space=pltpu.VMEM)
    out_shapes = [(3, 7, 8, 16, 128), (3, 7, 4, 8, 64), (3, 7, 2, 4, 32), (3, 2, 4, 32)]
    v = pltpu.VMEM
    scratch = [v((3, 29, 32, 256), F32), v((4, 3, 32, 256), F32)]
    scratch += [v((3, ZH[l], NX[l] + 11, NY[l] + 2 * ROWS[l], 128), F32) for l in range(3)]
    scratch += [v((3, ZH[l], 2, NX[l] // 2, NY[l] + 24, 128), F32) for l in range(3)]
    scratch += [v((4, ZH[l], 3 * NX[l] * NY[l] // 4, 128), F32) for l in range(3)]
    scratch += [v((8, 32, 128), F32), v((9, 3, 2, 4, 128), F32)]
    scratch += [v((4 if l < 2 else 5, NY[l] + 2 * ROWS[l], 128), F32) for l in range(3)]
    scratch += [v((2, DR[l], 128), F32) for l in range(3)]
    scratch += [v((NX[l] * NY[l] // 4, 128), F32) for l in range(3)]
    scratch += [v((32, 128), F32), v((32, 128), F32), v((1, 256), F32)]
    scratch += [v((256, 384), BF16), v((128, 384), BF16), v((128, 384), BF16)]
    scratch += [pltpu.SemaphoreType.DMA((96,)), pltpu.SemaphoreType.DMA((96,)), pltpu.SemaphoreType.DMA((8,))]
    results = pl.pallas_call(
        kernel,
        out_shape=[v(shape, F32) for shape in out_shapes],
        in_specs=[anywhere, smem, smem, smem, smem, vmem, anywhere, anywhere, anywhere],
        out_specs=[vmem] * 4,
        scratch_shapes=scratch,
        compiler_params=pltpu.CompilerParams(collective_id=0, has_side_effects=True),
        name="analysis",
    )(velocity, refine_flags, metric_table, index_x, index_y, index_z.reshape(1, 256), *weights)
    return pl.pallas_call(
        write_out,
        out_shape=[jax.ShapeDtypeStruct(shape, F32) for shape in out_shapes],
        in_specs=[vmem] * 4,
        out_specs=[anywhere] * 4,
        scratch_shapes=[pltpu.SemaphoreType.DMA((4,))],
        name="write_out",
    )(*[pltpu.with_memory_space_constraint(result, pltpu.VMEM) for result in results])


def solution(mesh):
    return jax.shard_map(
        on_device,
        mesh=mesh,
        in_specs=(P(None, "gx", "gy", None), P(None, "gx", "gy"), P(), P("gx"), P("gy"), P()),
        out_specs=(
            P(None, None, "gx", "gy", None),
            P(None, None, "gx", "gy", None),
            P(None, None, "gx", "gy", None),
            P(None, "gx", "gy", None),
        ),
        check_vma=False,
    )
```

```python
import functools

import jax
import jax.numpy as jnp
import numpy as np
from jax import lax
from jax.experimental import pallas as pl
from jax.experimental.pallas import tpu as pltpu
from jax.sharding import PartitionSpec as P

F32 = jnp.float32
BF16 = jnp.bfloat16
NX = (16, 8, 4)
NY = (32, 16, 8)
ZH = (2, 1, 1)
REP = (4, 2, 1)
DR = (24, 16, 8)
XK_LOW = (-1, -1, -2)
ROWS = (0, 8, 8)


def slot(sx, sy):
    return 3 * (sx + 1) + sy + 1


def z_matrices(count):
    half = count // 2
    even = np.zeros((count, half))
    residual = np.zeros((count, half))
    for k in range(half):
        even[2 * k, k] = 1.0
        residual[2 * k + 1, k] += 1.0
        for at, weight in ((k, -9), (k + 1, -9), (k - 1, 1), (k + 2, 1)):
            residual[2 * (at % half), k] += weight / 16.0
    update = np.zeros((count, half))
    for k in range(half):
        for at, weight in ((k - 1, 9), (k, 9), (k - 2, -1), (k + 1, -1)):
            update[:, k] += weight / 32.0 * residual[:, at % half]
    rows = max(count, 128)
    full = np.zeros((rows, 3, 128))
    for part, matrix in enumerate((even, residual, update)):
        full[:count, part, :half] = matrix
    return full.reshape(rows, 384)


def kernel(
    vel_hbm, flags, table, ix, iy, iz_ref, w1_hbm, w2_hbm, w3_hbm,
    o1, o2, o3, oc,
    vel, hy, c1, c2, c3, x1, x2, x3, y1, y2, y3, dscr,
    mk, mx1, mx2, mx3, my1, my2, my3, mz1, mz2, mz3, mxt, myt, mzt,
    w1, w2, w3,
    send_sem, recv_sem, local_sem,
):
    C, X, Y = (c1, c2, c3), (x1, x2, x3), (y1, y2, y3)
    MX, MY, MZ, W = (mx1, mx2, mx3), (my1, my2, my3), (mz1, mz2, mz3), (w1, w2, w3)
    gx, gy = lax.axis_index("gx"), lax.axis_index("gy")
    nx, ny = lax.axis_size("gx"), lax.axis_size("gy")

    def at(dx, dy):
        return {"gx": lax.rem(gx + (nx + dx), nx), "gy": lax.rem(gy + (ny + dy), ny)}

    counter = [0]
    pending = []

    def remote(src, dst, device):
        n = counter[0]
        counter[0] += 1
        copy = pltpu.make_async_remote_copy(
            src_ref=src, dst_ref=dst, send_sem=send_sem.at[n], recv_sem=recv_sem.at[n],
            device_id=device, device_id_type=pl.DeviceIdType.MESH,
        )
        copy.start()
        pending.append(copy)
        return copy

    def wait_recv(copies):
        for copy in copies:
            copy.wait_recv()

    local = [
        pltpu.make_async_copy(vel_hbm, vel.at[:, pl.ds(7, 16)], local_sem.at[0]),
        pltpu.make_async_copy(w1_hbm, w1, local_sem.at[1]),
        pltpu.make_async_copy(w2_hbm, w2, local_sem.at[2]),
        pltpu.make_async_copy(w3_hbm, w3, local_sem.at[3]),
    ]
    for copy in local:
        copy.start()

    direct = ((1, 0), (-1, 0), (0, 1), (0, -1))
    diagonal = ((1, 1), (1, -1), (-1, 1), (-1, -1))
    barrier = pltpu.get_barrier_semaphore()
    for step in direct:
        pl.semaphore_signal(barrier, inc=1, device_id=at(*step), device_id_type=pl.DeviceIdType.MESH)

    own = slot(0, 0)
    for l in range(3):
        for bx in range(2):
            for by in range(4):
                mk[own, l, bx, pl.ds(by, 1), :] = jnp.full((1, 128), flags[l, bx, by].astype(F32), F32)
    for i in range(16):
        mxt[pl.ds(i + 6, 1), :] = jnp.full((1, 128), table[0, ix[i]], F32)

    pl.semaphore_wait(barrier, len(direct))

    def send_rows(dx, dy, place, line):
        start, size, to = ((0, 8, 24), (0, 16, 8), (8, 8, 0))[dx + 1]
        return remote(vel_hbm.at[:, pl.ds(start, size), line], hy.at[place, :, pl.ds(to, size)], at(dx, dy))

    own_rows = [send_rows(0, 1, 0, 31), send_rows(0, -1, 1, 0)]
    inner_rows = [[send_rows(dx, 0, place, line) for dx in (1, -1)] for place, line in ((3, 23), (2, 8))]
    metric_in = [
        remote(mxt.at[pl.ds(16, 6)], mxt.at[pl.ds(0, 6)], at(1, 0)),
        remote(mxt.at[pl.ds(6, 5)], mxt.at[pl.ds(22, 5)], at(-1, 0)),
    ]

    def send_flags(steps):
        return [remote(mk.at[own], mk.at[slot(-dx, -dy)], at(dx, dy)) for dx, dy in steps]

    flags_in = send_flags(direct)

    def send_planes(first, size):
        rows = pl.ds(first, size)
        copies = []
        for dx, start, to, count in ((1, 9, -7, 7), (-1, 0, 16, 6)):
            skip = 1 if dx > 0 else 0
            copies.append(remote(
                vel_hbm.at[pl.ds(1, 2), pl.ds(start, count), rows], vel.at[pl.ds(1, 2), pl.ds(to + 7, count), rows], at(dx, 0)))
            copies.append(remote(
                vel_hbm.at[0, pl.ds(start + skip, count - 1), rows], vel.at[0, pl.ds(to + skip + 7, count - 1), rows], at(dx, 0)))
        return copies

    outer = [send_planes(24, 8), send_planes(0, 8)]
    for j in range(32):
        myt[pl.ds(j, 1), :] = jnp.full((1, 128), table[1, iy[j]], F32)
    iz = iz_ref[...]

    def z_class(c, total):
        return jnp.where(iz == c, table[2, c], total)

    mzt[...] = lax.fori_loop(0, 64, z_class, jnp.zeros((1, 256), F32))


    row = lax.broadcasted_iota(jnp.int32, (8, 256), 0)

    def vorticity(lo, hi, tiles, halo):
        def body(i, carry):
            mx = jnp.concatenate([mxt[pl.ds(i + 6, 1), :]] * 2, axis=1)
            mz = mzt[...]
            for t in tiles:
                rows = slice(8 * t, 8 * t + 8)
                u, v, w = vel[0, i + 7, rows], vel[1, i + 7, rows], vel[2, i + 7, rows]
                my = jnp.concatenate([myt[rows, :]] * 2, axis=1)

                def along_y(f, c):
                    place = 0 if t == 0 else 3 if halo and t == 3 else None
                    first = vel[c, i + 7, 8 * t - 1 : 8 * t] if place is None else hy[place, c, pl.ds(i + 8, 1), :]
                    place = 1 if t == 3 else 2 if halo and t == 0 else None
                    last = vel[c, i + 7, 8 * t + 8 : 8 * t + 9] if place is None else hy[place, c, pl.ds(i + 8, 1), :]
                    before = jnp.where(row == 0, first, pltpu.roll(f, 1, 0))
                    after = jnp.where(row == 7, last, pltpu.roll(f, 7, 0))
                    return (after - before) * my

                def along_z(f):
                    return (pltpu.roll(f, 255, 1) - pltpu.roll(f, 1, 1)) * mz

                dv_dx = (vel[1, i + 8, rows] - vel[1, i + 6, rows]) * mx
                dw_dx = (vel[2, i + 8, rows] - vel[2, i + 6, rows]) * mx
                curl = (along_y(w, 2) - along_z(v), along_z(u) - dw_dx, dv_dx - along_y(u, 0))
                for c in range(3):
                    for h in range(2):
                        c1[c, h, i + 6, rows] = curl[c][:, 128 * h : 128 * (h + 1)]
            return carry

        lax.fori_loop(lo, hi, body, 0)

    def lift_x(l, comps, tiles):
        half = NX[l] // 2
        first, step, count = tiles

        def body(it, carry):
            h, t = it // count, first + step * lax.rem(it, count)
            rows = pl.ds(pl.multiple_of(t * 8, 8), 8)
            rows_to = pl.ds(pl.multiple_of(t * 8 + 8 - ROWS[l], 8), 8)
            for c in comps:
                p = lambda i: C[l][c, h, i + 6, rows, :]
                d = {}
                for k in range(-2, half + 1):
                    mask = MX[l][k // REP[l] - XK_LOW[l], rows, :]
                    d[k] = (p(2 * k + 1) - (9.0 * (p(2 * k) + p(2 * k + 2)) - (p(2 * k - 2) + p(2 * k + 4))) * 0.0625) * mask
                for k in range(half):
                    smooth = p(2 * k) + (9.0 * (d[k - 1] + d[k]) - (d[k - 2] + d[k + 1])) * 0.03125
                    X[l][c, h, 0, k, rows_to, :] = smooth
                    X[l][c, h, 1, k, rows_to, :] = d[k]
            return carry

        lax.fori_loop(0, ZH[l] * count, body, 0)

    def lift_y(l, c, a):
        half_x, n, r = NX[l] // 2, NY[l] // 2, DR[l]

        def body(h, carry):
            for k in range(half_x):
                line = lambda start, count: X[l][c, h, a, k, pl.ds(start + 8, count, stride=2), :]
                mask = MY[l][k // REP[l]]
                d = (line(-3, r) - (9.0 * (line(-4, r) + line(-2, r)) - (line(-6, r) + line(0, r))) * 0.0625) * mask
                dscr[k, 0:r] = d
                part = lambda s: dscr[k, s : s + n]
                own_part = part(2)
                smooth = line(0, n) + (9.0 * (part(1) + own_part) - (part(0) + part(3))) * 0.03125
                to = (c * half_x + k) * n
                Y[l][2 * a, h, to : to + n] = smooth
                Y[l][2 * a + 1, h, to : to + n] = own_part
            return carry

        lax.fori_loop(0, ZH[l], body, 0)

    def lift_z(l, ab):
        half_x, n = NX[l] // 2, NY[l] // 2
        acc = None
        for h in range(ZH[l]):
            x = Y[l][ab, h]
            weights = W[l][h * 128 : (h + 1) * 128, :]
            hi = x.astype(BF16)
            rest = x - hi.astype(F32)
            mid = rest.astype(BF16)
            low = (rest - mid.astype(F32)).astype(BF16)
            for piece in (low, mid, hi):
                term = jnp.dot(piece, weights, preferred_element_type=F32)
                acc = term if acc is None else acc + term
        mask = jnp.concatenate([MZ[l][...]] * 3, axis=0)
        smooth = acc[:, :128] + mask * acc[:, 256:]
        detail = mask * acc[:, 128:256]
        lanes = (128, 64, 32)[l]
        out = (o1, o2, o3)[l]
        for c in range(3):
            for k in range(half_x):
                rows = slice((c * half_x + k) * n, (c * half_x + k + 1) * n)
                out[c, 2 * ab, k] = detail[rows, :lanes]
                if ab > 0:
                    out[c, 2 * ab - 1, k] = smooth[rows, :lanes]
                elif l < 2:
                    C[l + 1][c, 0, k + 6, 8 : 8 + n] = smooth[rows]
                else:
                    oc[c, k] = smooth[rows, :lanes]

    def send_lines(c, a, forward):
        if forward:
            return remote(x1.at[c, :, a, :, pl.ds(34, 6)], x1.at[c, :, a, :, pl.ds(2, 6)], at(0, 1))
        return remote(x1.at[c, :, a, :, pl.ds(8, 5)], x1.at[c, :, a, :, pl.ds(40, 5)], at(0, -1))

    def send_around(l):
        n, m = NX[l], NY[l]
        if l == 1:
            planes = ((1, n - 6, 1), (1, n - 4, 4), (-1, 0, 3), (-1, 4, 1))
        else:
            planes = ((1, 0, 4), (2, 2, 1), (-1, 0, 3), (-2, 0, 1))
        rows = ((1, m - 6, 6), (-1, 0, 5))
        moves = [(dx, dy, i, ci, j, cj) for dx, i, ci in planes for dy, j, cj in rows]
        moves += [(dx, 0, i, ci, 0, m) for dx, i, ci in planes]
        moves += [(0, dy, 0, n, j, cj) for dy, j, cj in rows]
        copies = []
        for dx, dy, i, ci, j, cj in moves:
            src = C[l].at[:, 0, pl.ds(i + 6, ci), pl.ds(j + 8, cj)]
            dst = C[l].at[:, 0, pl.ds(i + 6 - dx * n, ci), pl.ds(j + 8 - dy * m, cj)]
            copies.append(remote(src, dst, at(dx, dy)))
        return copies

    everything = (0, 1, 2)
    corner_rows = []
    for place, copy in ((1, own_rows[1]), (0, own_rows[0])):
        copy.wait_recv()
        line = hy.at[place]
        corner_rows.append([
            remote(line.at[:, pl.ds(16, 8)], line.at[:, pl.ds(0, 8)], at(1, 0)),
            remote(line.at[:, pl.ds(8, 8)], line.at[:, pl.ds(24, 8)], at(-1, 0)),
        ])
    inner = send_planes(8, 16)
    local[0].wait()
    vorticity(1, 15, (3, 0, 1, 2), False)

    def masks(l):
        per = 2 * REP[l]
        low = -ROWS[l] // per
        for k in range(MX[l].shape[0]):
            bx = k + XK_LOW[l]
            for by in range(low, NY[l] // per - low):
                place = slot(-1 if bx < 0 else 1 if bx > 1 else 0, -1 if by < 0 else 1 if by > 3 else 0)
                value = jnp.broadcast_to(mk[place, l, bx % 2, pl.ds(by % 4, 1), :], (per, 128))
                MX[l][k, pl.ds((by - low) * per, per), :] = value
        n = NY[l] // 2
        for bx in range(2):
            for m in range(-2, DR[l] - 2):
                by = min(m // REP[l], 4)
                place = slot(0, -1 if by < 0 else 1 if by > 3 else 0)
                MY[l][bx, pl.ds(m + 2, 1), :] = mk[place, l, bx, pl.ds(by % 4, 1), :]
        for k in range(NX[l] // 2):
            MZ[l][k * n : (k + 1) * n] = MY[l][k // REP[l], 2 : 2 + n]

    wait_recv(metric_in + flags_in)
    masks(0)
    for copy in local[1:]:
        copy.wait()

    lines = [[], [], []]
    for n, t in enumerate((3, 0)):
        wait_recv(corner_rows[n] + inner_rows[n] + outer[n])
        vorticity(-6, 0, (t,), True)
        vorticity(0, 1, (t,), False)
        vorticity(15, 16, (t,), False)
        vorticity(16, 21, (t,), True)
        for c in everything:
            lift_x(0, (c,), (t, 0, 1))
            lines[c].append(send_lines(c, 0, t == 3))
    flags_in = send_flags(diagonal)
    wait_recv(inner)
    vorticity(-6, 0, (1, 2), True)
    vorticity(0, 1, (1, 2), False)
    vorticity(15, 16, (1, 2), False)
    vorticity(16, 21, (1, 2), True)
    for c in everything:
        lift_x(0, (c,), (1, 1, 2))
    for c in everything:
        wait_recv(lines[c])
        lift_y(0, c, 0)
    lift_z(0, 0)
    around2 = send_around(1)
    lines = [[send_lines(c, 1, forward) for forward in (True, False)] for c in everything]
    wait_recv(flags_in)
    masks(1)
    masks(2)
    lift_z(0, 1)
    wait_recv(around2)
    lift_x(1, everything, (0, 1, 4))
    for c in everything:
        lift_y(1, c, 0)
    lift_z(1, 0)
    around3 = send_around(2)
    for c in everything:
        lift_y(1, c, 1)
    for ab in range(1, 4):
        lift_z(1, ab)
    for c in everything:
        wait_recv(lines[c])
        lift_y(0, c, 1)
    lift_z(0, 2)
    lift_z(0, 3)
    wait_recv(around3)
    lift_x(2, everything, (0, 1, 3))
    for c in everything:
        for a in range(2):
            lift_y(2, c, a)
    for ab in range(4):
        lift_z(2, ab)
    for copy in pending:
        copy.wait_send()


def write_out(*refs):
    sem = refs[8]
    copies = [pltpu.make_async_copy(refs[n], refs[4 + n], sem.at[n]) for n in range(4)]
    for copy in copies:
        copy.start()
    for copy in copies:
        copy.wait()


def on_device(velocity, refine_flags, metric_table, index_x, index_y, index_z):
    weights = [jnp.asarray(z_matrices(count).astype(np.float32)).astype(BF16) for count in (256, 128, 64)]
    anywhere = pl.BlockSpec(memory_space=pl.ANY)
    smem = pl.BlockSpec(memory_space=pltpu.SMEM)
    vmem = pl.BlockSpec(memory_space=pltpu.VMEM)
    out_shapes = [(3, 7, 8, 16, 128), (3, 7, 4, 8, 64), (3, 7, 2, 4, 32), (3, 2, 4, 32)]
    v = pltpu.VMEM
    scratch = [v((3, 29, 32, 256), F32), v((4, 3, 32, 256), F32)]
    scratch += [v((3, ZH[l], NX[l] + 11, NY[l] + 2 * ROWS[l], 128), F32) for l in range(3)]
    scratch += [v((3, ZH[l], 2, NX[l] // 2, NY[l] + 24, 128), F32) for l in range(3)]
    scratch += [v((4, ZH[l], 3 * NX[l] * NY[l] // 4, 128), F32) for l in range(3)]
    scratch += [v((8, 32, 128), F32), v((9, 3, 2, 4, 128), F32)]
    scratch += [v((4 if l < 2 else 5, NY[l] + 2 * ROWS[l], 128), F32) for l in range(3)]
    scratch += [v((2, DR[l], 128), F32) for l in range(3)]
    scratch += [v((NX[l] * NY[l] // 4, 128), F32) for l in range(3)]
    scratch += [v((32, 128), F32), v((32, 128), F32), v((1, 256), F32)]
    scratch += [v((256, 384), BF16), v((128, 384), BF16), v((128, 384), BF16)]
    scratch += [pltpu.SemaphoreType.DMA((96,)), pltpu.SemaphoreType.DMA((96,)), pltpu.SemaphoreType.DMA((8,))]
    results = pl.pallas_call(
        kernel,
        out_shape=[v(shape, F32) for shape in out_shapes],
        in_specs=[anywhere, smem, smem, smem, smem, vmem, anywhere, anywhere, anywhere],
        out_specs=[vmem] * 4,
        scratch_shapes=scratch,
        compiler_params=pltpu.CompilerParams(collective_id=0, has_side_effects=True),
        name="analysis",
    )(velocity, refine_flags, metric_table, index_x, index_y, index_z.reshape(1, 256), *weights)
    return pl.pallas_call(
        write_out,
        out_shape=[jax.ShapeDtypeStruct(shape, F32) for shape in out_shapes],
        in_specs=[vmem] * 4,
        out_specs=[anywhere] * 4,
        scratch_shapes=[pltpu.SemaphoreType.DMA((4,))],
        name="write_out",
    )(*[pltpu.with_memory_space_constraint(result, pltpu.VMEM) for result in results])


def solution(mesh):
    return jax.shard_map(
        on_device,
        mesh=mesh,
        in_specs=(P(None, "gx", "gy", None), P(None, "gx", "gy"), P(), P("gx"), P("gy"), P()),
        out_specs=(
            P(None, None, "gx", "gy", None),
            P(None, None, "gx", "gy", None),
            P(None, None, "gx", "gy", None),
            P(None, "gx", "gy", None),
        ),
        check_vma=False,
    )
```

```python
import functools

import jax
import jax.numpy as jnp
import numpy as np
from jax import lax
from jax.experimental import pallas as pl
from jax.experimental.pallas import tpu as pltpu
from jax.sharding import PartitionSpec as P

F32 = jnp.float32
BF16 = jnp.bfloat16
NX = (16, 8, 4)
NY = (32, 16, 8)
ZH = (2, 1, 1)
REP = (4, 2, 1)
DR = (24, 16, 8)
XK_LOW = (-1, -1, -2)
ROWS = (0, 8, 8)


def slot(sx, sy):
    return 3 * (sx + 1) + sy + 1


def z_matrices(count):
    half = count // 2
    even = np.zeros((count, half))
    residual = np.zeros((count, half))
    for k in range(half):
        even[2 * k, k] = 1.0
        residual[2 * k + 1, k] += 1.0
        for at, weight in ((k, -9), (k + 1, -9), (k - 1, 1), (k + 2, 1)):
            residual[2 * (at % half), k] += weight / 16.0
    update = np.zeros((count, half))
    for k in range(half):
        for at, weight in ((k - 1, 9), (k, 9), (k - 2, -1), (k + 1, -1)):
            update[:, k] += weight / 32.0 * residual[:, at % half]
    rows = max(count, 128)
    full = np.zeros((rows, 3, 128))
    for part, matrix in enumerate((even, residual, update)):
        full[:count, part, :half] = matrix
    return full.reshape(rows, 384)


def kernel(
    vel_hbm, flags, table, ix, iy, iz_ref, w1_hbm, w2_hbm, w3_hbm,
    o1, o2, o3, oc,
    vel, hy, c1, c2, c3, x1, x2, x3, y1, y2, y3, dscr,
    mk, mx1, mx2, mx3, my1, my2, my3, mz1, mz2, mz3, mxt, myt, mzt,
    w1, w2, w3,
    send_sem, recv_sem, local_sem,
):
    C, X, Y = (c1, c2, c3), (x1, x2, x3), (y1, y2, y3)
    MX, MY, MZ, W = (mx1, mx2, mx3), (my1, my2, my3), (mz1, mz2, mz3), (w1, w2, w3)
    gx, gy = lax.axis_index("gx"), lax.axis_index("gy")
    nx, ny = lax.axis_size("gx"), lax.axis_size("gy")

    def at(dx, dy):
        return {"gx": lax.rem(gx + (nx + dx), nx), "gy": lax.rem(gy + (ny + dy), ny)}

    counter = [0]
    pending = []

    def remote(src, dst, device):
        n = counter[0]
        counter[0] += 1
        copy = pltpu.make_async_remote_copy(
            src_ref=src, dst_ref=dst, send_sem=send_sem.at[n], recv_sem=recv_sem.at[n],
            device_id=device, device_id_type=pl.DeviceIdType.MESH,
        )
        copy.start()
        pending.append(copy)
        return copy

    def wait_recv(copies):
        for copy in copies:
            copy.wait_recv()

    direct = ((1, 0), (-1, 0), (0, 1), (0, -1))
    diagonal = ((1, 1), (1, -1), (-1, 1), (-1, -1))
    barrier = pltpu.get_barrier_semaphore()
    for step in direct:
        pl.semaphore_signal(barrier, inc=1, device_id=at(*step), device_id_type=pl.DeviceIdType.MESH)

    local = [
        pltpu.make_async_copy(vel_hbm, vel.at[:, pl.ds(7, 16)], local_sem.at[0]),
        pltpu.make_async_copy(w1_hbm, w1, local_sem.at[1]),
        pltpu.make_async_copy(w2_hbm, w2, local_sem.at[2]),
        pltpu.make_async_copy(w3_hbm, w3, local_sem.at[3]),
    ]
    for copy in local:
        copy.start()

    own = slot(0, 0)
    for l in range(3):
        for bx in range(2):
            for by in range(4):
                mk[own, l, bx, pl.ds(by, 1), :] = jnp.full((1, 128), flags[l, bx, by].astype(F32), F32)
    for i in range(16):
        mxt[pl.ds(i + 6, 1), :] = jnp.full((1, 128), table[0, ix[i]], F32)

    pl.semaphore_wait(barrier, len(direct))

    def send_rows(dx, dy, place, line):
        start, size, to = ((0, 8, 24), (0, 16, 8), (8, 8, 0))[dx + 1]
        return remote(vel_hbm.at[:, pl.ds(start, size), line], hy.at[place, :, pl.ds(to, size)], at(dx, dy))

    own_rows = [send_rows(0, 1, 0, 31), send_rows(0, -1, 1, 0)]
    inner_rows = [[send_rows(dx, 0, place, line) for dx in (1, -1)] for place, line in ((3, 23), (2, 8))]
    metric_in = [
        remote(mxt.at[pl.ds(16, 6)], mxt.at[pl.ds(0, 6)], at(1, 0)),
        remote(mxt.at[pl.ds(6, 5)], mxt.at[pl.ds(22, 5)], at(-1, 0)),
    ]

    def send_flags(steps):
        return [remote(mk.at[own], mk.at[slot(-dx, -dy)], at(dx, dy)) for dx, dy in steps]

    flags_in = send_flags(direct)

    def send_planes(first, size):
        rows = pl.ds(first, size)
        copies = []
        for dx, start, to, count in ((1, 9, -7, 7), (-1, 0, 16, 6)):
            skip = 1 if dx > 0 else 0
            copies.append(remote(
                vel_hbm.at[pl.ds(1, 2), pl.ds(start, count), rows], vel.at[pl.ds(1, 2), pl.ds(to + 7, count), rows], at(dx, 0)))
            copies.append(remote(
                vel_hbm.at[0, pl.ds(start + skip, count - 1), rows], vel.at[0, pl.ds(to + skip + 7, count - 1), rows], at(dx, 0)))
        return copies

    outer = [send_planes(24, 8), send_planes(0, 8)]
    for j in range(32):
        myt[pl.ds(j, 1), :] = jnp.full((1, 128), table[1, iy[j]], F32)
    iz = iz_ref[...]

    def z_class(c, total):
        return jnp.where(iz == c, table[2, c], total)

    mzt[...] = lax.fori_loop(0, 64, z_class, jnp.zeros((1, 256), F32))


    row = lax.broadcasted_iota(jnp.int32, (8, 256), 0)

    def vorticity(lo, hi, tiles, halo):
        def body(i, carry):
            mx = jnp.concatenate([mxt[pl.ds(i + 6, 1), :]] * 2, axis=1)
            mz = mzt[...]
            for t in tiles:
                rows = slice(8 * t, 8 * t + 8)
                u, v, w = vel[0, i + 7, rows], vel[1, i + 7, rows], vel[2, i + 7, rows]
                my = jnp.concatenate([myt[rows, :]] * 2, axis=1)

                def along_y(f, c):
                    place = 0 if t == 0 else 3 if halo and t == 3 else None
                    first = vel[c, i + 7, 8 * t - 1 : 8 * t] if place is None else hy[place, c, pl.ds(i + 8, 1), :]
                    place = 1 if t == 3 else 2 if halo and t == 0 else None
                    last = vel[c, i + 7, 8 * t + 8 : 8 * t + 9] if place is None else hy[place, c, pl.ds(i + 8, 1), :]
                    before = jnp.where(row == 0, first, pltpu.roll(f, 1, 0))
                    after = jnp.where(row == 7, last, pltpu.roll(f, 7, 0))
                    return (after - before) * my

                def along_z(f):
                    return (pltpu.roll(f, 255, 1) - pltpu.roll(f, 1, 1)) * mz

                dv_dx = (vel[1, i + 8, rows] - vel[1, i + 6, rows]) * mx
                dw_dx = (vel[2, i + 8, rows] - vel[2, i + 6, rows]) * mx
                curl = (along_y(w, 2) - along_z(v), along_z(u) - dw_dx, dv_dx - along_y(u, 0))
                for c in range(3):
                    for h in range(2):
                        c1[c, h, i + 6, rows] = curl[c][:, 128 * h : 128 * (h + 1)]
            return carry

        if len(tiles) < 4:
            for i in range(lo, hi):
                body(i, 0)
        else:
            lax.fori_loop(lo, hi, body, 0)

    def lift_x(l, comps, tiles):
        half = NX[l] // 2
        first, step, count = tiles

        def body(it, carry):
            h, t = it // count, first + step * (it % count)
            rows = pl.ds(t * 8 if isinstance(t, int) else pl.multiple_of(t * 8, 8), 8)
            to = t * 8 + 8 - ROWS[l]
            rows_to = pl.ds(to if isinstance(t, int) else pl.multiple_of(to, 8), 8)
            for c in comps:
                p = lambda i: C[l][c, h, i + 6, rows, :]
                d = {}
                for k in range(-2, half + 1):
                    mask = MX[l][k // REP[l] - XK_LOW[l], rows, :]
                    d[k] = (p(2 * k + 1) - (9.0 * (p(2 * k) + p(2 * k + 2)) - (p(2 * k - 2) + p(2 * k + 4))) * 0.0625) * mask
                for k in range(half):
                    smooth = p(2 * k) + (9.0 * (d[k - 1] + d[k]) - (d[k - 2] + d[k + 1])) * 0.03125
                    X[l][c, h, 0, k, rows_to, :] = smooth
                    X[l][c, h, 1, k, rows_to, :] = d[k]
            return carry

        if l > 0 or count == 1:
            for it in range(ZH[l] * count):
                body(it, 0)
        else:
            lax.fori_loop(0, ZH[l] * count, body, 0)

    def lift_y(l, c, a):
        half_x, n, r = NX[l] // 2, NY[l] // 2, DR[l]

        def body(h, carry):
            for k in range(half_x):
                line = lambda start, count: X[l][c, h, a, k, pl.ds(start + 8, count, stride=2), :]
                mask = MY[l][k // REP[l]]
                d = (line(-3, r) - (9.0 * (line(-4, r) + line(-2, r)) - (line(-6, r) + line(0, r))) * 0.0625) * mask
                place = k if l == 0 else 8 * l + (2 * c + a) * half_x + k
                dscr[place, 0:r] = d
                part = lambda s: dscr[place, s : s + n]
                own_part = part(2)
                smooth = line(0, n) + (9.0 * (part(1) + own_part) - (part(0) + part(3))) * 0.03125
                to = (c * half_x + k) * n
                Y[l][2 * a, h, to : to + n] = smooth
                Y[l][2 * a + 1, h, to : to + n] = own_part
            return carry

        if l > 0:
            body(0, 0)
        else:
            lax.fori_loop(0, 2, body, 0)

    def lift_z(l, ab, comps=(0, 1, 2)):
        half_x, n = NX[l] // 2, NY[l] // 2
        size = half_x * n
        parts = (ab,) if isinstance(ab, int) else ab
        acc = None
        for h in range(ZH[l]):
            x = jnp.concatenate([Y[l][ab, h, comps[0] * size : (comps[-1] + 1) * size, :] for ab in parts], axis=0)
            weights = W[l][h * 128 : (h + 1) * 128, :]
            hi = x.astype(BF16)
            rest = x - hi.astype(F32)
            mid = rest.astype(BF16)
            low = (rest - mid.astype(F32)).astype(BF16)
            for piece in (low, mid, hi):
                term = jnp.dot(piece, weights, preferred_element_type=F32)
                acc = term if acc is None else acc + term
        times = len(comps) * len(parts)
        mask = MZ[l][...] if times == 1 else jnp.concatenate([MZ[l][...]] * times, axis=0)
        smooth = acc[:, :128] + mask * acc[:, 256:]
        detail = mask * acc[:, 128:256]
        lanes = (128, 64, 32)[l]
        out = (o1, o2, o3)[l]
        for place, (ab, c) in enumerate([(ab, c) for ab in parts for c in comps]):
            for k in range(half_x):
                rows = slice((place * half_x + k) * n, (place * half_x + k + 1) * n)
                out[c, 2 * ab, k] = detail[rows, :lanes]
                if ab > 0:
                    out[c, 2 * ab - 1, k] = smooth[rows, :lanes]
                elif l < 2:
                    C[l + 1][c, 0, k + 6, 8 : 8 + n] = smooth[rows]
                else:
                    oc[c, k] = smooth[rows, :lanes]

    def send_lines(c, a, forward):
        if forward:
            return remote(x1.at[c, :, a, :, pl.ds(34, 6)], x1.at[c, :, a, :, pl.ds(2, 6)], at(0, 1))
        return remote(x1.at[c, :, a, :, pl.ds(8, 5)], x1.at[c, :, a, :, pl.ds(40, 5)], at(0, -1))

    def send_around(l):
        n, m = NX[l], NY[l]
        if l == 1:
            planes = ((1, n - 6, 1), (1, n - 4, 4), (-1, 0, 3), (-1, 4, 1))
        else:
            planes = ((1, 0, 4), (2, 2, 1), (-1, 0, 3), (-2, 0, 1))
        rows = ((1, m - 6, 6), (-1, 0, 5))
        moves = [(dx, dy, i, ci, j, cj) for dx, i, ci in planes for dy, j, cj in rows]
        moves += [(dx, 0, i, ci, 0, m) for dx, i, ci in planes]
        moves += [(0, dy, 0, n, j, cj) for dy, j, cj in rows]
        copies = []
        for dx, dy, i, ci, j, cj in moves:
            src = C[l].at[:, 0, pl.ds(i + 6, ci), pl.ds(j + 8, cj)]
            dst = C[l].at[:, 0, pl.ds(i + 6 - dx * n, ci), pl.ds(j + 8 - dy * m, cj)]
            copies.append(remote(src, dst, at(dx, dy)))
        return copies

    everything = (0, 1, 2)
    corner_rows = []
    for place, copy in ((1, own_rows[1]), (0, own_rows[0])):
        copy.wait_recv()
        line = hy.at[place]
        corner_rows.append([
            remote(line.at[:, pl.ds(16, 8)], line.at[:, pl.ds(0, 8)], at(1, 0)),
            remote(line.at[:, pl.ds(8, 8)], line.at[:, pl.ds(24, 8)], at(-1, 0)),
        ])
    inner = send_planes(8, 16)
    local[0].wait()
    vorticity(1, 15, (3, 0, 1, 2), False)

    def masks(l):
        per = 2 * REP[l]
        low = -ROWS[l] // per
        for k in range(MX[l].shape[0]):
            bx = k + XK_LOW[l]
            for by in range(low, NY[l] // per - low):
                place = slot(-1 if bx < 0 else 1 if bx > 1 else 0, -1 if by < 0 else 1 if by > 3 else 0)
                value = jnp.broadcast_to(mk[place, l, bx % 2, pl.ds(by % 4, 1), :], (per, 128))
                MX[l][k, pl.ds((by - low) * per, per), :] = value
        n = NY[l] // 2
        for bx in range(2):
            for m in range(-2, DR[l] - 2):
                by = min(m // REP[l], 4)
                place = slot(0, -1 if by < 0 else 1 if by > 3 else 0)
                MY[l][bx, pl.ds(m + 2, 1), :] = mk[place, l, bx, pl.ds(by % 4, 1), :]
        for k in range(NX[l] // 2):
            MZ[l][k * n : (k + 1) * n] = MY[l][k // REP[l], 2 : 2 + n]

    wait_recv(metric_in + flags_in)
    masks(0)
    for copy in local[1:]:
        copy.wait()

    lines = [[], [], []]
    for n, t in enumerate((3, 0)):
        wait_recv(corner_rows[n] + inner_rows[n] + outer[n])
        vorticity(-6, 0, (t,), True)
        vorticity(0, 1, (t,), False)
        vorticity(15, 16, (t,), False)
        vorticity(16, 21, (t,), True)
        for c in everything:
            lift_x(0, (c,), (t, 0, 1))
            lines[c].append(send_lines(c, 0, t == 3))
    flags_in = send_flags(diagonal)
    detail_lines = [[send_lines(c, 1, forward) for forward in (True, False)] for c in everything]
    wait_recv(inner)
    vorticity(-6, 0, (1, 2), True)
    vorticity(0, 1, (1, 2), False)
    vorticity(15, 16, (1, 2), False)
    vorticity(16, 21, (1, 2), True)
    for c in everything:
        lift_x(0, (c,), (1, 1, 2))
    for c in everything:
        wait_recv(lines[c])
        lift_y(0, c, 0)
        lift_z(0, 0, (c,))
    around2 = send_around(1)
    wait_recv(flags_in)
    masks(1)
    masks(2)
    lift_z(0, 1)
    wait_recv(around2)
    lift_x(1, everything, (0, 1, 4))
    for c in everything:
        lift_y(1, c, 0)
    lift_z(1, 0)
    around3 = send_around(2)
    for c in everything:
        lift_y(1, c, 1)
    lift_z(1, (1, 2, 3))
    for c in everything:
        wait_recv(detail_lines[c])
        lift_y(0, c, 1)
    lift_z(0, 2)
    lift_z(0, 3)
    wait_recv(around3)
    lift_x(2, everything, (0, 1, 3))
    for c in everything:
        for a in range(2):
            lift_y(2, c, a)
    lift_z(2, (0, 1, 2, 3))
    for copy in pending:
        copy.wait_send()


def write_out(*refs):
    sem = refs[8]
    copies = [pltpu.make_async_copy(refs[n], refs[4 + n], sem.at[n]) for n in range(4)]
    for copy in copies:
        copy.start()
    for copy in copies:
        copy.wait()


def on_device(velocity, refine_flags, metric_table, index_x, index_y, index_z):
    weights = [jnp.asarray(z_matrices(count).astype(np.float32)).astype(BF16) for count in (256, 128, 64)]
    anywhere = pl.BlockSpec(memory_space=pl.ANY)
    smem = pl.BlockSpec(memory_space=pltpu.SMEM)
    vmem = pl.BlockSpec(memory_space=pltpu.VMEM)
    out_shapes = [(3, 7, 8, 16, 128), (3, 7, 4, 8, 64), (3, 7, 2, 4, 32), (3, 2, 4, 32)]
    v = pltpu.VMEM
    scratch = [v((3, 29, 32, 256), F32), v((4, 3, 32, 256), F32)]
    scratch += [v((3, ZH[l], NX[l] + 11, NY[l] + 2 * ROWS[l], 128), F32) for l in range(3)]
    scratch += [v((3, ZH[l], 2, NX[l] // 2, NY[l] + 24, 128), F32) for l in range(3)]
    scratch += [v((4, ZH[l], 3 * NX[l] * NY[l] // 4, 128), F32) for l in range(3)]
    scratch += [v((40, 32, 128), F32), v((9, 3, 2, 4, 128), F32)]
    scratch += [v((4 if l < 2 else 5, NY[l] + 2 * ROWS[l], 128), F32) for l in range(3)]
    scratch += [v((2, DR[l], 128), F32) for l in range(3)]
    scratch += [v((NX[l] * NY[l] // 4, 128), F32) for l in range(3)]
    scratch += [v((32, 128), F32), v((32, 128), F32), v((1, 256), F32)]
    scratch += [v((256, 384), BF16), v((128, 384), BF16), v((128, 384), BF16)]
    scratch += [pltpu.SemaphoreType.DMA((96,)), pltpu.SemaphoreType.DMA((96,)), pltpu.SemaphoreType.DMA((8,))]
    results = pl.pallas_call(
        kernel,
        out_shape=[v(shape, F32) for shape in out_shapes],
        in_specs=[anywhere, smem, smem, smem, smem, vmem, anywhere, anywhere, anywhere],
        out_specs=[vmem] * 4,
        scratch_shapes=scratch,
        compiler_params=pltpu.CompilerParams(collective_id=0, has_side_effects=True),
        name="analysis",
    )(velocity, refine_flags, metric_table, index_x, index_y, index_z.reshape(1, 256), *weights)
    return pl.pallas_call(
        write_out,
        out_shape=[jax.ShapeDtypeStruct(shape, F32) for shape in out_shapes],
        in_specs=[vmem] * 4,
        out_specs=[anywhere] * 4,
        scratch_shapes=[pltpu.SemaphoreType.DMA((4,))],
        name="write_out",
    )(*[pltpu.with_memory_space_constraint(result, pltpu.VMEM) for result in results])


def solution(mesh):
    return jax.shard_map(
        on_device,
        mesh=mesh,
        in_specs=(P(None, "gx", "gy", None), P(None, "gx", "gy"), P(), P("gx"), P("gy"), P()),
        out_specs=(
            P(None, None, "gx", "gy", None),
            P(None, None, "gx", "gy", None),
            P(None, None, "gx", "gy", None),
            P(None, "gx", "gy", None),
        ),
        check_vma=False,
    )
```

```python
import functools

import jax
import jax.numpy as jnp
import numpy as np
from jax import lax
from jax.experimental import pallas as pl
from jax.experimental.pallas import tpu as pltpu
from jax.sharding import PartitionSpec as P

F32 = jnp.float32
BF16 = jnp.bfloat16
NX = (16, 8, 4)
NY = (32, 16, 8)
ZH = (2, 1, 1)
REP = (4, 2, 1)
DR = (24, 16, 8)
XK_LOW = (-1, -1, -2)
ROWS = (0, 8, 8)


def slot(sx, sy):
    return 3 * (sx + 1) + sy + 1


def z_matrices(count):
    half = count // 2
    even = np.zeros((count, half))
    residual = np.zeros((count, half))
    for k in range(half):
        even[2 * k, k] = 1.0
        residual[2 * k + 1, k] += 1.0
        for at, weight in ((k, -9), (k + 1, -9), (k - 1, 1), (k + 2, 1)):
            residual[2 * (at % half), k] += weight / 16.0
    update = np.zeros((count, half))
    for k in range(half):
        for at, weight in ((k - 1, 9), (k, 9), (k - 2, -1), (k + 1, -1)):
            update[:, k] += weight / 32.0 * residual[:, at % half]
    rows = max(count, 128)
    full = np.zeros((rows, 3, 128))
    for part, matrix in enumerate((even, residual, update)):
        full[:count, part, :half] = matrix
    return full.reshape(rows, 384)


def kernel(
    vel_hbm, flags_hbm, table_hbm, ix_hbm, iy_hbm, iz_hbm, w1_hbm, w2_hbm, w3_hbm,
    o1, o2, o3, oc,
    vel, hy, c1, c2, c3, x1, x2, x3, y1, y2, y3, dscr,
    mk, mx1, mx2, mx3, my1, my2, my3, mz1, mz2, mz3, mxt, myt, mzt,
    w1, w2, w3, flags, table, ix, iy, iz_ref,
    send_sem, recv_sem, local_sem,
):
    C, X, Y = (c1, c2, c3), (x1, x2, x3), (y1, y2, y3)
    MX, MY, MZ, W = (mx1, mx2, mx3), (my1, my2, my3), (mz1, mz2, mz3), (w1, w2, w3)
    gx, gy = lax.axis_index("gx"), lax.axis_index("gy")
    nx, ny = lax.axis_size("gx"), lax.axis_size("gy")

    def at(dx, dy):
        return {"gx": lax.rem(gx + (nx + dx), nx), "gy": lax.rem(gy + (ny + dy), ny)}

    counter = [0]
    pending = []

    def remote(src, dst, device):
        n = counter[0]
        counter[0] += 1
        copy = pltpu.make_async_remote_copy(
            src_ref=src, dst_ref=dst, send_sem=send_sem.at[n], recv_sem=recv_sem.at[n],
            device_id=device, device_id_type=pl.DeviceIdType.MESH,
        )
        copy.start()
        pending.append(copy)
        return copy

    def wait_recv(copies):
        for copy in copies:
            copy.wait_recv()

    direct = ((1, 0), (-1, 0), (0, 1), (0, -1))
    diagonal = ((1, 1), (1, -1), (-1, 1), (-1, -1))
    barrier = pltpu.get_barrier_semaphore()
    for step in direct:
        pl.semaphore_signal(barrier, inc=1, device_id=at(*step), device_id_type=pl.DeviceIdType.MESH)

    small = [
        pltpu.make_async_copy(src, dst, local_sem.at[n])
        for n, (src, dst) in enumerate(
            ((flags_hbm, flags), (table_hbm, table), (ix_hbm, ix), (iy_hbm, iy), (iz_hbm, iz_ref)), 4
        )
    ]
    for copy in small:
        copy.start()
    local = [
        pltpu.make_async_copy(vel_hbm, vel.at[:, pl.ds(7, 16)], local_sem.at[0]),
        pltpu.make_async_copy(w1_hbm, w1, local_sem.at[1]),
        pltpu.make_async_copy(w2_hbm, w2, local_sem.at[2]),
        pltpu.make_async_copy(w3_hbm, w3, local_sem.at[3]),
    ]
    for copy in local:
        copy.start()

    for copy in small:
        copy.wait()
    own = slot(0, 0)
    for l in range(3):
        for bx in range(2):
            for by in range(4):
                mk[own, l, bx, pl.ds(by, 1), :] = jnp.full((1, 128), flags[l, bx, by].astype(F32), F32)
    for i in range(16):
        mxt[pl.ds(i + 6, 1), :] = jnp.full((1, 128), table[0, ix[i]], F32)

    pl.semaphore_wait(barrier, len(direct))

    def send_rows(dx, dy, place, line):
        start, size, to = ((0, 8, 24), (0, 16, 8), (8, 8, 0))[dx + 1]
        return remote(vel_hbm.at[:, pl.ds(start, size), line], hy.at[place, :, pl.ds(to, size)], at(dx, dy))

    own_rows = [send_rows(0, 1, 0, 31), send_rows(0, -1, 1, 0)]
    inner_rows = [[send_rows(dx, 0, place, line) for dx in (1, -1)] for place, line in ((3, 23), (2, 8))]
    metric_in = [
        remote(mxt.at[pl.ds(16, 6)], mxt.at[pl.ds(0, 6)], at(1, 0)),
        remote(mxt.at[pl.ds(6, 5)], mxt.at[pl.ds(22, 5)], at(-1, 0)),
    ]

    def send_flags(steps):
        return [remote(mk.at[own], mk.at[slot(-dx, -dy)], at(dx, dy)) for dx, dy in steps]

    flags_in = send_flags(direct)

    def send_planes(first, size):
        rows = pl.ds(first, size)
        copies = []
        for dx, start, to, count in ((1, 9, -7, 7), (-1, 0, 16, 6)):
            skip = 1 if dx > 0 else 0
            copies.append(remote(
                vel_hbm.at[pl.ds(1, 2), pl.ds(start, count), rows], vel.at[pl.ds(1, 2), pl.ds(to + 7, count), rows], at(dx, 0)))
            copies.append(remote(
                vel_hbm.at[0, pl.ds(start + skip, count - 1), rows], vel.at[0, pl.ds(to + skip + 7, count - 1), rows], at(dx, 0)))
        return copies

    outer = [send_planes(24, 8), send_planes(0, 8)]
    for j in range(32):
        myt[pl.ds(j, 1), :] = jnp.full((1, 128), table[1, iy[j]], F32)
    iz = iz_ref[...]

    def z_class(c, total):
        return jnp.where(iz == c, table[2, c], total)

    mzt[...] = lax.fori_loop(0, 64, z_class, jnp.zeros((1, 256), F32))


    row = lax.broadcasted_iota(jnp.int32, (8, 256), 0)

    def vorticity(lo, hi, tiles, halo):
        def body(i, carry):
            mx = jnp.concatenate([mxt[pl.ds(i + 6, 1), :]] * 2, axis=1)
            mz = mzt[...]
            for t in tiles:
                rows = slice(8 * t, 8 * t + 8)
                u, v, w = vel[0, i + 7, rows], vel[1, i + 7, rows], vel[2, i + 7, rows]
                my = jnp.concatenate([myt[rows, :]] * 2, axis=1)

                def along_y(f, c):
                    place = 0 if t == 0 else 3 if halo and t == 3 else None
                    first = vel[c, i + 7, 8 * t - 1 : 8 * t] if place is None else hy[place, c, pl.ds(i + 8, 1), :]
                    place = 1 if t == 3 else 2 if halo and t == 0 else None
                    last = vel[c, i + 7, 8 * t + 8 : 8 * t + 9] if place is None else hy[place, c, pl.ds(i + 8, 1), :]
                    before = jnp.where(row == 0, first, pltpu.roll(f, 1, 0))
                    after = jnp.where(row == 7, last, pltpu.roll(f, 7, 0))
                    return (after - before) * my

                def along_z(f):
                    return (pltpu.roll(f, 255, 1) - pltpu.roll(f, 1, 1)) * mz

                dv_dx = (vel[1, i + 8, rows] - vel[1, i + 6, rows]) * mx
                dw_dx = (vel[2, i + 8, rows] - vel[2, i + 6, rows]) * mx
                curl = (along_y(w, 2) - along_z(v), along_z(u) - dw_dx, dv_dx - along_y(u, 0))
                for c in range(3):
                    for h in range(2):
                        c1[c, h, i + 6, rows] = curl[c][:, 128 * h : 128 * (h + 1)]
            return carry

        if len(tiles) < 4:
            for i in range(lo, hi):
                body(i, 0)
        else:
            lax.fori_loop(lo, hi, body, 0)

    def lift_x(l, comps, tiles):
        half = NX[l] // 2
        first, step, count = tiles

        def body(it, carry):
            h, t = it // count, first + step * (it % count)
            rows = pl.ds(t * 8 if isinstance(t, int) else pl.multiple_of(t * 8, 8), 8)
            to = t * 8 + 8 - ROWS[l]
            rows_to = pl.ds(to if isinstance(t, int) else pl.multiple_of(to, 8), 8)
            for c in comps:
                p = lambda i: C[l][c, h, i + 6, rows, :]
                d = {}
                for k in range(-2, half + 1):
                    mask = MX[l][k // REP[l] - XK_LOW[l], rows, :]
                    d[k] = (p(2 * k + 1) - (9.0 * (p(2 * k) + p(2 * k + 2)) - (p(2 * k - 2) + p(2 * k + 4))) * 0.0625) * mask
                for k in range(half):
                    smooth = p(2 * k) + (9.0 * (d[k - 1] + d[k]) - (d[k - 2] + d[k + 1])) * 0.03125
                    X[l][c, h, 0, k, rows_to, :] = smooth
                    X[l][c, h, 1, k, rows_to, :] = d[k]
            return carry

        if l > 0 or count == 1:
            for it in range(ZH[l] * count):
                body(it, 0)
        else:
            lax.fori_loop(0, ZH[l] * count, body, 0)

    def lift_y(l, c, a):
        half_x, n, r = NX[l] // 2, NY[l] // 2, DR[l]

        def body(h, carry):
            for k in range(half_x):
                line = lambda start, count: X[l][c, h, a, k, pl.ds(start + 8, count, stride=2), :]
                mask = MY[l][k // REP[l]]
                d = (line(-3, r) - (9.0 * (line(-4, r) + line(-2, r)) - (line(-6, r) + line(0, r))) * 0.0625) * mask
                place = k if l == 0 else 8 * l + (2 * c + a) * half_x + k
                dscr[place, 0:r] = d
                part = lambda s: dscr[place, s : s + n]
                own_part = part(2)
                smooth = line(0, n) + (9.0 * (part(1) + own_part) - (part(0) + part(3))) * 0.03125
                to = (c * half_x + k) * n
                Y[l][2 * a, h, to : to + n] = smooth
                Y[l][2 * a + 1, h, to : to + n] = own_part
            return carry

        if l > 0:
            body(0, 0)
        else:
            lax.fori_loop(0, 2, body, 0)

    def lift_z(l, ab, comps=(0, 1, 2)):
        half_x, n = NX[l] // 2, NY[l] // 2
        size = half_x * n
        parts = (ab,) if isinstance(ab, int) else ab
        acc = None
        for h in range(ZH[l]):
            x = jnp.concatenate([Y[l][ab, h, comps[0] * size : (comps[-1] + 1) * size, :] for ab in parts], axis=0)
            weights = W[l][h * 128 : (h + 1) * 128, :]
            hi = x.astype(BF16)
            rest = x - hi.astype(F32)
            mid = rest.astype(BF16)
            low = (rest - mid.astype(F32)).astype(BF16)
            for piece in (low, mid, hi):
                term = jnp.dot(piece, weights, preferred_element_type=F32)
                acc = term if acc is None else acc + term
        times = len(comps) * len(parts)
        mask = MZ[l][...] if times == 1 else jnp.concatenate([MZ[l][...]] * times, axis=0)
        smooth = acc[:, :128] + mask * acc[:, 256:]
        detail = mask * acc[:, 128:256]
        lanes = (128, 64, 32)[l]
        out = (o1, o2, o3)[l]
        for place, (ab, c) in enumerate([(ab, c) for ab in parts for c in comps]):
            for k in range(half_x):
                rows = slice((place * half_x + k) * n, (place * half_x + k + 1) * n)
                out[c, 2 * ab, k] = detail[rows, :lanes]
                if ab > 0:
                    out[c, 2 * ab - 1, k] = smooth[rows, :lanes]
                elif l < 2:
                    C[l + 1][c, 0, k + 6, 8 : 8 + n] = smooth[rows]
                else:
                    oc[c, k] = smooth[rows, :lanes]

    def send_lines(c, a, forward):
        if forward:
            return remote(x1.at[c, :, a, :, pl.ds(34, 6)], x1.at[c, :, a, :, pl.ds(2, 6)], at(0, 1))
        return remote(x1.at[c, :, a, :, pl.ds(8, 5)], x1.at[c, :, a, :, pl.ds(40, 5)], at(0, -1))

    def send_around(l):
        n, m = NX[l], NY[l]
        if l == 1:
            planes = ((1, n - 6, 1), (1, n - 4, 4), (-1, 0, 3), (-1, 4, 1))
        else:
            planes = ((1, 0, 4), (2, 2, 1), (-1, 0, 3), (-2, 0, 1))
        rows = ((1, m - 6, 6), (-1, 0, 5))
        moves = [(dx, dy, i, ci, j, cj) for dx, i, ci in planes for dy, j, cj in rows]
        moves += [(dx, 0, i, ci, 0, m) for dx, i, ci in planes]
        moves += [(0, dy, 0, n, j, cj) for dy, j, cj in rows]
        copies = []
        for dx, dy, i, ci, j, cj in moves:
            src = C[l].at[:, 0, pl.ds(i + 6, ci), pl.ds(j + 8, cj)]
            dst = C[l].at[:, 0, pl.ds(i + 6 - dx * n, ci), pl.ds(j + 8 - dy * m, cj)]
            copies.append(remote(src, dst, at(dx, dy)))
        return copies

    everything = (0, 1, 2)
    corner_rows = []
    for place, copy in ((1, own_rows[1]), (0, own_rows[0])):
        copy.wait_recv()
        line = hy.at[place]
        corner_rows.append([
            remote(line.at[:, pl.ds(16, 8)], line.at[:, pl.ds(0, 8)], at(1, 0)),
            remote(line.at[:, pl.ds(8, 8)], line.at[:, pl.ds(24, 8)], at(-1, 0)),
        ])
    inner = send_planes(8, 16)
    local[0].wait()
    vorticity(1, 15, (3, 0, 1, 2), False)

    def masks(l):
        per = 2 * REP[l]
        low = -ROWS[l] // per
        for k in range(MX[l].shape[0]):
            bx = k + XK_LOW[l]
            for by in range(low, NY[l] // per - low):
                place = slot(-1 if bx < 0 else 1 if bx > 1 else 0, -1 if by < 0 else 1 if by > 3 else 0)
                value = jnp.broadcast_to(mk[place, l, bx % 2, pl.ds(by % 4, 1), :], (per, 128))
                MX[l][k, pl.ds((by - low) * per, per), :] = value
        n = NY[l] // 2
        for bx in range(2):
            for m in range(-2, DR[l] - 2):
                by = min(m // REP[l], 4)
                place = slot(0, -1 if by < 0 else 1 if by > 3 else 0)
                MY[l][bx, pl.ds(m + 2, 1), :] = mk[place, l, bx, pl.ds(by % 4, 1), :]
        for k in range(NX[l] // 2):
            MZ[l][k * n : (k + 1) * n] = MY[l][k // REP[l], 2 : 2 + n]

    wait_recv(metric_in + flags_in)
    masks(0)
    for copy in local[1:]:
        copy.wait()

    lines = [[], [], []]
    for n, t in enumerate((3, 0)):
        wait_recv(corner_rows[n] + inner_rows[n] + outer[n])
        vorticity(-6, 0, (t,), True)
        vorticity(0, 1, (t,), False)
        vorticity(15, 16, (t,), False)
        vorticity(16, 21, (t,), True)
        for c in everything:
            lift_x(0, (c,), (t, 0, 1))
            lines[c].append(send_lines(c, 0, t == 3))
    flags_in = send_flags(diagonal)
    detail_lines = [[send_lines(c, 1, forward) for forward in (True, False)] for c in everything]
    wait_recv(inner)
    vorticity(-6, 0, (1, 2), True)
    vorticity(0, 1, (1, 2), False)
    vorticity(15, 16, (1, 2), False)
    vorticity(16, 21, (1, 2), True)
    for c in everything:
        lift_x(0, (c,), (1, 1, 2))
    for c in everything:
        wait_recv(lines[c])
        lift_y(0, c, 0)
        lift_z(0, 0, (c,))
    around2 = send_around(1)
    wait_recv(flags_in)
    masks(1)
    masks(2)
    lift_z(0, 1)
    for c in everything:
        wait_recv(detail_lines[c])
        lift_y(0, c, 1)
    lift_z(0, 2)
    wait_recv(around2[8:12])
    lift_x(1, everything, (1, 1, 2))
    wait_recv(around2[:8] + around2[12:])
    lift_x(1, everything, (0, 3, 2))
    for c in everything:
        lift_y(1, c, 0)
    lift_z(1, 0)
    around3 = send_around(2)
    for c in everything:
        lift_y(1, c, 1)
    lift_z(1, (1, 2, 3))
    lift_z(0, 3)
    for copy in pending[:-14]:
        copy.wait_send()
    wait_recv(around3[8:12])
    lift_x(2, everything, (1, 1, 1))
    wait_recv(around3[:8] + around3[12:])
    lift_x(2, everything, (0, 2, 2))
    for c in everything:
        for a in range(2):
            lift_y(2, c, a)
    lift_z(2, (0, 1, 2, 3))
    for copy in pending[-14:]:
        copy.wait_send()


def write_out(*refs):
    sem = refs[8]
    copies = [pltpu.make_async_copy(refs[n], refs[4 + n], sem.at[n]) for n in range(4)]
    for copy in copies:
        copy.start()
    for copy in copies:
        copy.wait()


def on_device(velocity, refine_flags, metric_table, index_x, index_y, index_z):
    weights = [jnp.asarray(z_matrices(count).astype(np.float32)).astype(BF16) for count in (256, 128, 64)]
    anywhere = pl.BlockSpec(memory_space=pl.ANY)
    vmem = pl.BlockSpec(memory_space=pltpu.VMEM)
    out_shapes = [(3, 7, 8, 16, 128), (3, 7, 4, 8, 64), (3, 7, 2, 4, 32), (3, 2, 4, 32)]
    v = pltpu.VMEM
    scratch = [v((3, 29, 32, 256), F32), v((4, 3, 32, 256), F32)]
    scratch += [v((3, ZH[l], NX[l] + 11, NY[l] + 2 * ROWS[l], 128), F32) for l in range(3)]
    scratch += [v((3, ZH[l], 2, NX[l] // 2, NY[l] + 24, 128), F32) for l in range(3)]
    scratch += [v((4, ZH[l], 3 * NX[l] * NY[l] // 4, 128), F32) for l in range(3)]
    scratch += [v((40, 32, 128), F32), v((9, 3, 2, 4, 128), F32)]
    scratch += [v((4 if l < 2 else 5, NY[l] + 2 * ROWS[l], 128), F32) for l in range(3)]
    scratch += [v((2, DR[l], 128), F32) for l in range(3)]
    scratch += [v((NX[l] * NY[l] // 4, 128), F32) for l in range(3)]
    scratch += [v((32, 128), F32), v((32, 128), F32), v((1, 256), F32)]
    scratch += [v((256, 384), BF16), v((128, 384), BF16), v((128, 384), BF16)]
    i32 = jnp.int32
    scratch += [pltpu.SMEM((3, 2, 4), i32), pltpu.SMEM((3, 64), F32), pltpu.SMEM((16,), i32), pltpu.SMEM((32,), i32), v((1, 256), i32)]
    scratch += [pltpu.SemaphoreType.DMA((96,)), pltpu.SemaphoreType.DMA((96,)), pltpu.SemaphoreType.DMA((9,))]
    results = pl.pallas_call(
        kernel,
        out_shape=[v(shape, F32) for shape in out_shapes],
        in_specs=[anywhere] * 9,
        out_specs=[vmem] * 4,
        scratch_shapes=scratch,
        compiler_params=pltpu.CompilerParams(collective_id=0, has_side_effects=True),
        name="analysis",
    )(velocity, refine_flags, metric_table, index_x, index_y, index_z.reshape(1, 256), *weights)
    return pl.pallas_call(
        write_out,
        out_shape=[jax.ShapeDtypeStruct(shape, F32) for shape in out_shapes],
        in_specs=[vmem] * 4,
        out_specs=[anywhere] * 4,
        scratch_shapes=[pltpu.SemaphoreType.DMA((4,))],
        name="write_out",
    )(*[pltpu.with_memory_space_constraint(result, pltpu.VMEM) for result in results])


def solution(mesh):
    return jax.shard_map(
        on_device,
        mesh=mesh,
        in_specs=(P(None, "gx", "gy", None), P(None, "gx", "gy"), P(), P("gx"), P("gy"), P()),
        out_specs=(
            P(None, None, "gx", "gy", None),
            P(None, None, "gx", "gy", None),
            P(None, None, "gx", "gy", None),
            P(None, "gx", "gy", None),
        ),
        check_vma=False,
    )
```
